256 devices in a mesh: space: 16 (over y, x_hi, core), offset: 16 (over z, x_lo).
Axes of the slice: x: 4 (x_hi: 2, x_lo: 2; x = x_hi * 2 + x_lo), y: 4, z: 8, core: 2. Of those that a mesh axis runs over, the one named last changes fastest.
Arguments:
- src_prev: float32 [4, 256, 2048], P(None, 'offset', 'space'), may hold values from -6 to 6
- src_now: float32 [4, 256, 2048], P(None, 'offset', 'space'), may hold values from -6 to 6
- rcv_prev: float32 [4, 256, 2048], P(None, 'offset', 'space'), may hold values from -6 to 6
- rcv_now: float32 [4, 256, 2048], P(None, 'offset', 'space'), may hold values from -6 to 6
- velocity: float32 [4, 256, 2048], P(None, 'offset', 'space'), may hold values from 0.03 to 0.16
- shift_table: int32 [256, 2], P('offset'), may hold values from -8 to 7, as said below
- ref_image: bfloat16 [256, 4, 256, 2048], P('offset', None, None, 'space'), may hold values from -6 to 6
Outputs:
- image: bfloat16 [256, 4, 256, 2048], P('offset', None, None, 'space')
- adjoint: float32 [4, 256, 2048], P(None, 'offset', 'space')
The draws below stay inside these ranges and needn't reach their ends.
Inputs may be any that keep to these rules, and one draw needn't show every extreme that they name: `shift_table`: each row is (hx, hy); every pair with both entries in the range appears exactly once, in an order drawn from the seed.
All inputs are finite; a program needn't handle non-finite values.
Results may differ from the reference program's by a relative error of at most 0.001.
Values sent between devices are 32-bit elements; how exact they have to be, the bound alone decides.
No kernel may reach another device: no remote copies, remote signals or barrier semaphores. Data moves between devices by JAX's collectives and lax.ppermute only.
A program may use at most 64 MiB of HBM per device.

```python
import math
import jax
import jax.numpy as jnp
from jax import lax

Z = 4
OFF_SIDE = 16
STEPS = 2
NOFF = 256
HMAX = 8
NX = 2048
NY = 256


def draw_shift_table(key, part):
    order = jax.random.permutation(key, NOFF).astype(jnp.int32)
    shift_x = order % OFF_SIDE - HMAX
    shift_y = order // OFF_SIDE - HMAX
    return jnp.stack([shift_x, shift_y], axis=1).astype(jnp.int32)


def steps_of(stream_key, shape, pieces, low, high):
    loudness = 1.0
    for axis_at, shards_of in pieces:
        heights = jax.random.uniform(jax.random.fold_in(jax.random.fold_in(stream_key, 6), axis_at), (shards_of,), jnp.float32, low / len(pieces), high / len(pieces))
        loudness = loudness * jnp.repeat(jnp.exp(heights), shape[axis_at] // shards_of).reshape((-1,) + (1,) * (len(shape) - 1 - axis_at))
    return loudness


def bell_draw(rng, dims, scale, bound, pieces=(), held_as=jnp.bfloat16):
    values = scale * jax.random.normal(rng, dims, jnp.float32)
    if pieces:
        values = values * steps_of(rng, dims, pieces, -0.22, 0.18)
    return jnp.clip(values, -bound, bound).astype(held_as)


def setup_inputs(seed: int = 0) -> dict:
    key_of = jax.random.split(jax.random.key(seed), 8)
    return {
        "src_prev": bell_draw(key_of[0], (Z, NY, NX), 1.0, 6.0, ((1, 16), (2, 16)), jnp.float32),
        "src_now": bell_draw(key_of[1], (Z, NY, NX), 1.0, 6.0, ((1, 16), (2, 16)), jnp.float32),
        "rcv_prev": bell_draw(key_of[2], (Z, NY, NX), 1.0, 6.0, ((1, 16), (2, 16)), jnp.float32),
        "rcv_now": bell_draw(key_of[3], (Z, NY, NX), 1.0, 6.0, ((1, 16), (2, 16)), jnp.float32),
        "velocity": jnp.clip(jnp.exp(math.log(0.16) - 1.6739764 * jax.random.uniform(key_of[4], (Z, NY, NX), jnp.float32) ** steps_of(key_of[4], (Z, NY, NX), ((1, 16), (2, 16)), -0.2, 0.2)), 0.03, 0.16),
        "shift_table": draw_shift_table(jax.random.fold_in(key_of[7], 71), 0),
        "ref_image": bell_draw(key_of[6], (NOFF, Z, NY, NX), 1.0, 6.0, ((0, 16), (3, 16))),
    }


def laplace(field):
    padded = jnp.pad(field, 1)
    beside = padded[2:, 1:-1, 1:-1] + padded[:-2, 1:-1, 1:-1]
    beside = beside + padded[1:-1, 2:, 1:-1] + padded[1:-1, :-2, 1:-1]
    beside = beside + padded[1:-1, 1:-1, 2:] + padded[1:-1, 1:-1, :-2]
    return beside - 6.0 * field


def reference(src_prev, src_now, rcv_prev, rcv_now, velocity, shift_table, ref_image):
    snaps = []
    for step in range(STEPS):
        src_next = 2.0 * src_now - src_prev + velocity * laplace(src_now)
        rcv_next = 2.0 * rcv_now - rcv_prev + velocity * laplace(rcv_now)
        src_prev, src_now = src_now, src_next
        rcv_prev, rcv_now = rcv_now, rcv_next
        widths = ((0, 0), (HMAX, HMAX), (HMAX, HMAX))
        snaps.append((jnp.pad(src_now, widths), jnp.pad(rcv_now, widths)))
    zero_index = jnp.zeros((), jnp.int32)

    def per_offset(carry, inputs):
        row, observed = inputs
        shift_x = row[0].astype(jnp.int32)
        shift_y = row[1].astype(jnp.int32)
        full = jnp.zeros((Z, NY, NX), jnp.float32)
        source_shifted = full
        for src_pad, rcv_pad in snaps:
            source_shifted = lax.dynamic_slice(src_pad, (zero_index, (HMAX - shift_y).astype(jnp.int32), (HMAX - shift_x).astype(jnp.int32)), (Z, NY, NX))
            rcv_shifted = lax.dynamic_slice(rcv_pad, (zero_index, (HMAX + shift_y).astype(jnp.int32), (HMAX + shift_x).astype(jnp.int32)), (Z, NY, NX))
            full = full + source_shifted * rcv_shifted
        misfit = full - observed.astype(jnp.float32)
        term = misfit * source_shifted
        starts = (zero_index, (HMAX + shift_y).astype(jnp.int32), (HMAX + shift_x).astype(jnp.int32))
        window = lax.dynamic_slice(carry, starts, (Z, NY, NX))
        carry = lax.dynamic_update_slice(carry, window + term, starts)
        return carry, full.astype(jnp.bfloat16)

    start = jnp.zeros((Z, NY + 2 * HMAX, NX + 2 * HMAX), jnp.float32)
    carry, image = lax.scan(per_offset, start, (shift_table, ref_image))
    adjoint = carry[:, HMAX:HMAX + NY, HMAX:HMAX + NX] / OFF_SIDE
    return image, adjoint
```

```python
import jax
import jax.numpy as jnp
from jax import lax
from jax.experimental import pallas as pl
from jax.experimental.pallas import tpu as pltpu
from jax.sharding import PartitionSpec as P

OFF_SIDE = 16
HMAX = 8
STEPS = 2
REACH = HMAX + STEPS
LANES = 128


def chain(count):
    forward = [(i, i + 1) for i in range(count - 1)]
    return forward, [(b, a) for a, b in forward]


def roll_lanes(x, shift):
    return pltpu.roll(x, shift, x.ndim - 1)


def wave_kernel(u_ref, tile_ref):
    depth = u_ref.shape[1]
    rows = tile_ref.shape[1]
    high_rows, width = u_ref.shape[2], u_ref.shape[3]
    lane = lax.broadcasted_iota(jnp.int32, (rows, LANES), 1)
    speed = [u_ref[4, z] for z in range(depth)]

    def advance(prev, now):
        out = []
        for z in range(depth):
            c = now[z]
            beside = pltpu.roll(c, 1, 0) + pltpu.roll(c, high_rows - 1, 0)
            beside = beside + roll_lanes(c, 1) + roll_lanes(c, width - 1)
            if z > 0:
                beside = beside + now[z - 1]
            if z < depth - 1:
                beside = beside + now[z + 1]
            out.append(2.0 * c - prev[z] + speed[z] * (beside - 6.0 * c))
        return out

    packed = [jnp.zeros((rows, LANES), jnp.float32) for _ in range(2)]
    for pair in range(2):
        prev = [u_ref[2 * pair, z] for z in range(depth)]
        now = [u_ref[2 * pair + 1, z] for z in range(depth)]
        for t in range(STEPS):
            prev, now = now, advance(prev, now)
            for z in range(depth):
                plane = (pair * STEPS + t) * depth + z
                tile_ref[plane] = now[z][:rows, :LANES]
                q = plane % 8
                beside = roll_lanes(now[z][:rows, LANES:], (8 + 16 * q) % LANES)
                here = (lane >= 16 * q) & (lane < 16 * q + 16)
                packed[plane // 8] = jnp.where(here, beside, packed[plane // 8])
    for k in range(2):
        tile_ref[4 * depth + k] = packed[k]


def image_kernel(place_ref, shifts_ref, *refs):
    tiles = refs[:8]
    ref_ref, image_ref, adj_ref, main, side, acc, acc_side = refs[8:]
    step = pl.program_id(0)
    depth, all_rows = ref_ref.shape[1], ref_ref.shape[2]
    rows = tiles[0].shape[2]
    planes = 4 * depth

    @pl.when(step == 0)
    def _():
        zeros = jnp.zeros((planes, HMAX, LANES), jnp.float32)
        for edge in (0, HMAX + all_rows):
            main[:, edge:edge + HMAX, :] = zeros
            side[:, edge:edge + HMAX, :] = zeros
        acc[...] = jnp.zeros_like(acc)
        acc_side[...] = jnp.zeros_like(acc_side)
        for r in range(8):
            z_at = lax.rem(place_ref[0] + r, 8)
            for half in range(2):
                start = pl.multiple_of(HMAX + (2 * z_at + half) * rows, 8)
                for p in range(planes):
                    main[p, pl.ds(start, rows), :] = tiles[r][half, p]
                    packed = tiles[r][half, planes + p // 8]
                    back = (-(8 + 16 * (p % 8))) % LANES
                    side[p, pl.ds(start, rows), :] = roll_lanes(packed, back)

    hx = shifts_ref[step, 0]
    hy = shifts_ref[step, 1]
    block = 64
    lane = lax.broadcasted_iota(jnp.int32, (block, LANES), 1)
    wrap_s = (lane < -hx) | (lane >= LANES - hx)
    wrap_r = (lane < hx) | (lane >= LANES + hx)
    to_s = lax.rem(hx + LANES, LANES)
    to_r = lax.rem(LANES - hx, LANES)

    def rows_of(at, carry):
        z = at // (all_rows // block)
        r0 = pl.multiple_of(lax.rem(at, all_rows // block) * block, block)
        s_at = r0 + HMAX - hy
        r_at = r0 + HMAX + hy

        def shifted(plane, start, wrap, amount):
            a = main[plane, pl.ds(start, block), :]
            b = side[plane, pl.ds(start, block), :]
            return pltpu.roll(jnp.where(wrap, b, a), amount, 1)

        s1 = shifted(z, s_at, wrap_s, to_s)
        r1 = shifted(2 * depth + z, r_at, wrap_r, to_r)
        s2 = shifted(depth + z, s_at, wrap_s, to_s)
        r2 = shifted(3 * depth + z, r_at, wrap_r, to_r)
        full = s1 * r1 + s2 * r2
        image_ref[0, z, pl.ds(r0, block), :] = full.astype(jnp.bfloat16)
        observed = ref_ref[0, z, pl.ds(r0, block), :].astype(jnp.float32)
        term = pltpu.roll((full - observed) * s2, to_s, 1)
        acc[z, pl.ds(r_at, block), :] += jnp.where(wrap_r, 0.0, term)
        acc_side[z, pl.ds(r_at, block), :] += jnp.where(wrap_r, term, 0.0)
        return carry

    lax.fori_loop(0, depth * (all_rows // block), rows_of, 0)

    @pl.when(step == pl.num_programs(0) - 1)
    def _():
        lane8 = lax.broadcasted_iota(jnp.int32, (8, LANES), 1)
        for tile in range(all_rows // rows):
            strip = jnp.zeros((8, LANES), jnp.float32)
            for z in range(depth):
                at = HMAX + tile * rows
                adj_ref[tile, z * rows:(z + 1) * rows, :] = acc[z, at:at + rows, :]
                for half in range(2):
                    q = half * 4 + z
                    part = acc_side[z, at + 8 * half:at + 8 * half + 8, :]
                    part = pltpu.roll(part, (8 + 16 * q) % LANES, 1)
                    here = (lane8 >= 16 * q) & (lane8 < 16 * q + 16)
                    strip = jnp.where(here, part, strip)
            adj_ref[tile, depth * rows:, :] = strip


def total_kernel(parts_ref, core_ref, strip_ref):
    total = parts_ref[0]
    for i in range(1, parts_ref.shape[0]):
        total = total + parts_ref[i]
    n = core_ref.shape[0]
    core_ref[...] = total[:n]
    strip_ref[...] = total[n:]


def finish_kernel(core_ref, left_ref, right_ref, out_ref):
    depth, rows = out_ref.shape[0], out_ref.shape[1]
    lane = lax.broadcasted_iota(jnp.int32, (8, LANES), 1)
    for z in range(depth):
        for half in range(2):
            q = half * 4 + z
            back = (-(8 + 16 * q)) % LANES
            from_left = pltpu.roll(left_ref[...], back, 1)
            from_right = pltpu.roll(right_ref[...], back, 1)
            extra = jnp.where(lane < HMAX, from_left, 0.0)
            extra = jnp.where(lane >= LANES - HMAX, from_right, extra)
            at = z * rows + 8 * half
            out_ref[z, 8 * half:8 * half + 8, :] = (core_ref[at:at + 8, :] + extra) / OFF_SIDE


def on_device(src_prev, src_now, rcv_prev, rcv_now, velocity, shift_table, ref_image):
    depth, rows, cols = src_now.shape
    n_off = lax.axis_size("offset")
    n_space = lax.axis_size("space")
    all_rows = ref_image.shape[2]
    raw = jnp.stack([src_prev, src_now, rcv_prev, rcv_now, velocity])
    forward, backward = chain(n_space)
    low = lax.ppermute(raw[..., cols - REACH:], "space", forward)
    high = lax.ppermute(raw[..., :REACH], "space", backward)
    gap = jnp.zeros(raw.shape[:-1] + (LANES - 2 * REACH,), jnp.float32)
    wide = jnp.concatenate([raw, high, gap, low], axis=-1)
    forward, backward = chain(n_off)
    top = lax.ppermute(wide[:, :, rows - STEPS:], "offset", forward)
    bottom = lax.ppermute(wide[:, :, :STEPS], "offset", backward)
    gap = jnp.zeros(wide.shape[:2] + (8 - 2 * STEPS,) + wide.shape[3:], jnp.float32)
    wide = jnp.concatenate([wide, bottom, gap, top], axis=2)
    planes = 4 * depth + 2
    tile = pl.pallas_call(
        wave_kernel,
        out_shape=jax.ShapeDtypeStruct((planes, rows, LANES), jnp.float32),
        name="wave",
    )(wide)

    me = lax.axis_index("offset")
    other = lax.ppermute(tile, "offset", [(i, i ^ 1) for i in range(n_off)])
    is_low = (me % 2) == 0
    pair = jnp.stack([jnp.where(is_low, tile, other), jnp.where(is_low, other, tile)])

    def turn(d):
        return [(i, (i - 2 * d) % n_off) for i in range(n_off)]

    tiles = [pair] + [None] * 7
    up = down = pair
    for d in range(1, 4):
        up = lax.ppermute(up, "offset", turn(1))
        down = lax.ppermute(down, "offset", turn(-1))
        tiles[d], tiles[8 - d] = up, down
    far_a = lax.ppermute(up[0], "offset", turn(1))
    far_b = lax.ppermute(down[1], "offset", turn(-1))
    tiles[4] = jnp.stack([far_a, far_b])

    local = shift_table.shape[0]
    place = (me // 2).astype(jnp.int32)[None]
    whole = pl.BlockSpec(memory_space=pltpu.VMEM)
    scalars = pl.BlockSpec(memory_space=pltpu.SMEM)
    per_offset = pl.BlockSpec((1, depth, all_rows, cols), lambda i: (i, 0, 0, 0))
    padded_rows = all_rows + 2 * HMAX
    image, parts = pl.pallas_call(
        image_kernel,
        grid=(local,),
        in_specs=[scalars, scalars] + [whole] * 8 + [per_offset],
        out_specs=[per_offset, pl.BlockSpec((n_off, (depth * rows) + 8, LANES), lambda i: (0, 0, 0))],
        out_shape=[
            jax.ShapeDtypeStruct(ref_image.shape, jnp.bfloat16),
            jax.ShapeDtypeStruct((n_off, depth * rows + 8, LANES), jnp.float32),
        ],
        scratch_shapes=[
            pltpu.VMEM((4 * depth, padded_rows, LANES), jnp.float32),
            pltpu.VMEM((4 * depth, padded_rows, LANES), jnp.float32),
            pltpu.VMEM((depth, padded_rows, LANES), jnp.float32),
            pltpu.VMEM((depth, padded_rows, LANES), jnp.float32),
        ],
        compiler_params=pltpu.CompilerParams(vmem_limit_bytes=48 * 2**20),
        name="image",
    )(place, shift_table, *tiles, ref_image)

    parts = lax.all_to_all(parts, "offset", 0, 0)
    core, strip = pl.pallas_call(
        total_kernel,
        out_shape=[
            jax.ShapeDtypeStruct((depth * rows, LANES), jnp.float32),
            jax.ShapeDtypeStruct((8, LANES), jnp.float32),
        ],
        name="total",
    )(parts)
    forward, backward = chain(n_space)
    left = lax.ppermute(strip, "space", forward)
    right = lax.ppermute(strip, "space", backward)
    adjoint = pl.pallas_call(
        finish_kernel,
        out_shape=jax.ShapeDtypeStruct((depth, rows, cols), jnp.float32),
        name="finish",
    )(core, left, right)
    return image, adjoint


def solution(mesh):
    field = P(None, "offset", "space")
    in_specs = (field,) * 5 + (P("offset", None), P("offset", None, None, "space"))
    out_specs = (P("offset", None, None, "space"), field)
    return jax.shard_map(
        on_device, mesh=mesh, in_specs=in_specs, out_specs=out_specs, check_vma=False
    )
```

```python
import functools

import jax
import jax.numpy as jnp
from jax import lax
from jax.experimental import pallas as pl
from jax.experimental.pallas import tpu as pltpu
from jax.sharding import PartitionSpec as P

OFF_SIDE = 16
HMAX = 8
STEPS = 2
REACH = HMAX + STEPS
LANES = 128
UNROLL = 2
SMALL = pltpu.CompilerParams(vmem_limit_bytes=6 * 2**20)


def chain(count):
    forward = [(i, i + 1) for i in range(count - 1)]
    return forward, [(b, a) for a, b in forward]


def roll_lanes(x, shift):
    return pltpu.roll(x, shift, x.ndim - 1)


def stack_kernel(*refs):
    out_ref = refs[-1]
    for i, ref in enumerate(refs[:-1]):
        out_ref[i] = ref[...]


def widen_kernel(raw_ref, low_ref, high_ref, wide_ref, upper_ref, lower_ref):
    fields, depth, rows, cols = raw_ref.shape
    lane = lax.broadcasted_iota(jnp.int32, (rows, cols), 1)
    for f in range(fields):
        for z in range(depth):
            beside = jnp.where(lane >= cols - REACH, low_ref[f, z], 0.0)
            beside = jnp.where(lane < REACH, high_ref[f, z], beside)
            row = raw_ref[f, z]
            wide_ref[f, z, :, :cols] = row
            wide_ref[f, z, :, cols:] = beside
            upper_ref[f, z, :, :cols] = row[:8]
            upper_ref[f, z, :, cols:] = beside[:8]
            lower_ref[f, z, :, :cols] = row[rows - 8:]
            lower_ref[f, z, :, cols:] = beside[rows - 8:]


def wave_kernel(wide_ref, top_ref, bottom_ref, tile_ref):
    depth, rows, width = wide_ref.shape[1:]
    high_rows = rows + 8
    lane = lax.broadcasted_iota(jnp.int32, (rows, LANES), 1)
    edge_row = lax.broadcasted_iota(jnp.int32, (8, width), 0)

    def whole(f, z):
        edge = jnp.where(edge_row >= 8 - STEPS, top_ref[f, z], 0.0)
        edge = jnp.where(edge_row < STEPS, bottom_ref[f, z], edge)
        return jnp.concatenate([wide_ref[f, z], edge], axis=0)

    speed = [whole(4, z) for z in range(depth)]

    def advance(prev, now):
        out = []
        for z in range(depth):
            c = now[z]
            beside = pltpu.roll(c, 1, 0) + pltpu.roll(c, high_rows - 1, 0)
            beside = beside + roll_lanes(c, 1) + roll_lanes(c, width - 1)
            if z > 0:
                beside = beside + now[z - 1]
            if z < depth - 1:
                beside = beside + now[z + 1]
            out.append(2.0 * c - prev[z] + speed[z] * (beside - 6.0 * c))
        return out

    packed = [jnp.zeros((rows, LANES), jnp.float32) for _ in range(2)]
    for pair in range(2):
        prev = [whole(2 * pair, z) for z in range(depth)]
        now = [whole(2 * pair + 1, z) for z in range(depth)]
        for t in range(STEPS):
            prev, now = now, advance(prev, now)
            for z in range(depth):
                plane = (pair * STEPS + t) * depth + z
                tile_ref[plane] = now[z][:rows, :LANES]
                q = plane % 8
                beside = roll_lanes(now[z][:rows, LANES:], (8 + 16 * q) % LANES)
                here = (lane >= 16 * q) & (lane < 16 * q + 16)
                packed[plane // 8] = jnp.where(here, beside, packed[plane // 8])
    for k in range(2):
        tile_ref[4 * depth + k] = packed[k]


def needed(rels):
    return sorted({(r + k) % 8 for r in rels for k in (-1, 0, 1)})


def image_kernel(rels, first, last, *refs):
    refs = list(refs)
    place_ref, shifts_ref, observed_ref = refs[:3]
    del refs[:3]
    tiles = {}
    for r in needed(rels):
        tiles[r], refs = refs[:2], refs[2:]
    if not first:
        refs = refs[1:]
    earlier = {}
    if last:
        for r in range(8):
            if r not in rels:
                earlier[r], refs = refs[:2], refs[2:]
    image_hbm, core_out, side_out, main, side, image_buf, sems = refs[:7]
    if last:
        acc, acc_side, all_core, all_side = refs[7:]
    else:
        acc, acc_side = core_out, side_out
    count, depth, all_rows = observed_ref.shape[:3]
    planes = 4 * depth
    rows = all_rows // 8
    half = rows // 2
    z_of = [lax.rem(place_ref[0] + r, 8) for r in rels]

    def put(n):
        at = pl.multiple_of(z_of[n] * rows, rows)
        return pltpu.make_async_copy(
            image_buf.at[n], image_hbm.at[:, :, pl.ds(at, rows), :], sems.at[n]
        )

    acc[...] = jnp.zeros_like(acc)
    acc_side[...] = jnp.zeros_like(acc_side)
    for n, r in enumerate(rels):
        below, here, above = tiles[(r - 1) % 8], tiles[r], tiles[(r + 1) % 8]
        sources = [
            (0, below[1], slice(half - HMAX, half), z_of[n] > 0),
            (HMAX, here[0], slice(0, half), None),
            (HMAX + half, here[1], slice(0, half), None),
            (HMAX + rows, above[0], slice(0, HMAX), z_of[n] < 7),
        ]
        for at, ref, part, inside in sources:
            size = part.stop - part.start

            def load(p):
                value = ref[p, part, :]
                return value if inside is None else jnp.where(inside, value, 0.0)

            packs = [load(planes), load(planes + 1)]
            for p in range(planes):
                main[n, p, at:at + size, :] = load(p)
                back = (-(8 + 16 * (p % 8))) % LANES
                side[n, p, at:at + size, :] = roll_lanes(packs[p // 8], back)

    lane = lax.broadcasted_iota(jnp.int32, (rows, LANES), 1)

    def per_offset(o, carry):
        hx = shifts_ref[o, 0]
        hy = shifts_ref[o, 1]
        wrap_s = (lane < -hx) | (lane >= LANES - hx)
        wrap_r = (lane < hx) | (lane >= LANES + hx)
        to_s = lax.rem(hx + LANES, LANES)
        to_r = lax.rem(LANES - hx, LANES)
        s_at = HMAX - hy
        r_at = HMAX + hy

        def rotated(pieces, amount):
            turned = pltpu.roll(jnp.concatenate(pieces, axis=0), amount, 1)
            return [turned[i * rows:(i + 1) * rows] for i in range(len(pieces))]

        def piece(n, plane, start, wrap):
            a = main[n, plane, pl.ds(start, rows), :]
            return jnp.where(wrap, side[n, plane, pl.ds(start, rows), :], a)

        parts = [(n, z) for n in range(len(rels)) for z in range(depth)]
        sources, receivers = [], []
        for n, z in parts:
            for t in range(STEPS):
                sources.append(piece(n, t * depth + z, s_at, wrap_s))
                receivers.append(piece(n, (STEPS + t) * depth + z, r_at, wrap_r))
        sources = rotated(sources, to_s)
        receivers = rotated(receivers, to_r)
        terms = []
        for i, (n, z) in enumerate(parts):
            s1, s2 = sources[2 * i:2 * i + 2]
            r1, r2 = receivers[2 * i:2 * i + 2]
            full = s1 * r1 + s2 * r2
            image_buf[n, o, z] = full.astype(jnp.bfloat16)
            y_at = pl.multiple_of(z_of[n] * rows, rows)
            observed = observed_ref[o, z, pl.ds(y_at, rows), :].astype(jnp.float32)
            terms.append((full - observed) * s2)
        terms = rotated(terms, to_s)
        spots = [(n, z, pl.ds(r_at, rows)) for n, z in parts]
        sums = [acc[at] + jnp.where(wrap_r, 0.0, t) for at, t in zip(spots, terms)]
        sides = [acc_side[at] + jnp.where(wrap_r, t, 0.0) for at, t in zip(spots, terms)]
        for at, v, w in zip(spots, sums, sides):
            acc[at] = v
            acc_side[at] = w
        return carry

    lax.fori_loop(0, count, per_offset, 0, unroll=UNROLL)
    for n in range(len(rels)):
        put(n).start()

    if last:
        all_core[...] = jnp.zeros_like(all_core)
        all_side[...] = jnp.zeros_like(all_side)
        window = rows + 2 * HMAX
        for r in range(8):
            at = pl.multiple_of(lax.rem(place_ref[0] + r, 8) * rows, rows)
            if r in rels:
                c, e = acc[rels.index(r)], acc_side[rels.index(r)]
            else:
                c, e = earlier[r][0][...], earlier[r][1][...]
            all_core[:, pl.ds(at, window), :] += c
            all_side[:, pl.ds(at, window), :] += e
        lane8 = lax.broadcasted_iota(jnp.int32, (8, LANES), 1)
        for tile in range(all_rows // half):
            strip = jnp.zeros((8, LANES), jnp.float32)
            at = HMAX + tile * half
            for z in range(depth):
                core_out[tile, z * half:(z + 1) * half, :] = all_core[z, at:at + half, :]
                for k in range(2):
                    q = k * 4 + z
                    part = all_side[z, at + 8 * k:at + 8 * k + 8, :]
                    part = pltpu.roll(part, (8 + 16 * q) % LANES, 1)
                    here = (lane8 >= 16 * q) & (lane8 < 16 * q + 16)
                    strip = jnp.where(here, part, strip)
            side_out[tile] = strip
    for n in range(len(rels)):
        put(n).wait()


def merge_kernel(core_ref, left_ref, right_ref, out_ref):
    lane = lax.broadcasted_iota(jnp.int32, (8, LANES), 1)
    for tile in range(core_ref.shape[0]):
        for q in range(8):
            back = (-(8 + 16 * q)) % LANES
            extra = jnp.where(lane < HMAX, pltpu.roll(left_ref[tile], back, 1), 0.0)
            from_right = pltpu.roll(right_ref[tile], back, 1)
            extra = jnp.where(lane >= LANES - HMAX, from_right, extra)
            at = (q % 4) * 16 + (q // 4) * 8
            out_ref[tile, at:at + 8, :] = core_ref[tile, at:at + 8, :] + extra


def total_kernel(parts_ref, out_ref):
    total = parts_ref[0]
    for i in range(1, parts_ref.shape[0]):
        total = total + parts_ref[i]
    rows = out_ref.shape[1]
    for z in range(out_ref.shape[0]):
        out_ref[z] = total[z * rows:(z + 1) * rows] * (1.0 / OFF_SIDE)


def on_device(src_prev, src_now, rcv_prev, rcv_now, velocity, shift_table, ref_image):
    depth, rows, cols = src_now.shape
    n_off = lax.axis_size("offset")
    n_space = lax.axis_size("space")
    all_rows = ref_image.shape[2]
    shape = jax.ShapeDtypeStruct
    f32 = jnp.float32
    raw = pl.pallas_call(
        stack_kernel, out_shape=shape((5, depth, rows, cols), f32), name="stack"
    )(src_prev, src_now, rcv_prev, rcv_now, velocity)
    forward, backward = chain(n_space)
    low = lax.ppermute(raw, "space", forward)
    high = lax.ppermute(raw, "space", backward)
    edge = shape((5, depth, 8, 2 * LANES), f32)
    wide, upper, lower = pl.pallas_call(
        widen_kernel,
        out_shape=[shape((5, depth, rows, 2 * LANES), f32), edge, edge],
        name="widen", compiler_params=SMALL,
    )(raw, low, high)
    forward_y, backward_y = chain(n_off)
    top = lax.ppermute(lower, "offset", forward_y)
    bottom = lax.ppermute(upper, "offset", backward_y)
    planes = 4 * depth + 2
    tile = pl.pallas_call(
        wave_kernel, out_shape=shape((planes, rows, LANES), f32), name="wave", compiler_params=SMALL
    )(wide, top, bottom)

    me = lax.axis_index("offset")
    other = lax.ppermute(tile, "offset", [(i, i ^ 1) for i in range(n_off)])
    is_low = (me % 2) == 0
    pair = jnp.stack([jnp.where(is_low, tile, other), jnp.where(is_low, other, tile)])

    def turn(d):
        return [(i, (i - 2 * d) % n_off) for i in range(n_off)]

    tiles = [(pair[0], pair[1])] + [None] * 7
    up = down = pair
    for d in range(1, 4):
        up = lax.ppermute(up, "offset", turn(1))
        down = lax.ppermute(down, "offset", turn(-1))
        tiles[d], tiles[8 - d] = (up[0], up[1]), (down[0], down[1])
    tiles[4] = (
        lax.ppermute(up[0], "offset", turn(1)),
        lax.ppermute(down[1], "offset", turn(-1)),
    )

    local = shift_table.shape[0]
    place = (me // 2).astype(jnp.int32)[None]
    whole = pl.BlockSpec(memory_space=pltpu.VMEM)
    scalars = pl.BlockSpec(memory_space=pltpu.SMEM)
    anywhere = pl.BlockSpec(memory_space=pl.ANY)
    window = all_rows // 8 + 2 * HMAX
    image = None
    done = {}
    for rels in ((0,), (1, 7), (2, 6), (3, 5, 4)):
        first, last = image is None, 4 in rels
        n = len(rels)
        chunk = (n, depth, window, LANES)
        args = [place, shift_table, ref_image]
        specs = [scalars, scalars, whole]
        for r in needed(rels):
            args += tiles[r]
            specs += [whole, whole]
        aliases = {}
        if not first:
            aliases = {len(args): 0}
            args.append(image)
            specs.append(anywhere)
        scratch = [
            pltpu.VMEM((n, 4 * depth, window, LANES), f32),
            pltpu.VMEM((n, 4 * depth, window, LANES), f32),
            pltpu.VMEM((n, local, depth, all_rows // 8, LANES), jnp.bfloat16),
            pltpu.SemaphoreType.DMA((n,)),
        ]
        if last:
            for r in range(8):
                if r not in rels:
                    args += done[r]
                    specs += [whole, whole]
            scratch += [pltpu.VMEM(chunk, f32)] * 2
            scratch += [pltpu.VMEM((depth, all_rows + 2 * HMAX, LANES), f32)] * 2
            outs = [shape((n_off, depth * rows, LANES), f32), shape((n_off, 8, LANES), f32)]
        else:
            outs = [shape(chunk, f32)] * 2
        image, core, strip = pl.pallas_call(
            functools.partial(image_kernel, rels, first, last),
            in_specs=specs,
            out_specs=[anywhere, whole, whole],
            out_shape=[shape(ref_image.shape, jnp.bfloat16)] + outs,
            scratch_shapes=scratch,
            input_output_aliases=aliases,
            compiler_params=pltpu.CompilerParams(vmem_limit_bytes=16 * 2**20),
            cost_estimate=pl.CostEstimate(
                flops=n * 10_000_000, bytes_accessed=n * 4_000_000, transcendentals=0
            ),
            name="image",
        )(*args)
        if not last:
            for i, r in enumerate(rels):
                done[r] = (core[i], strip[i])

    left = lax.ppermute(strip, "space", forward)
    right = lax.ppermute(strip, "space", backward)
    parts = pl.pallas_call(
        merge_kernel, out_shape=shape(core.shape, f32), name="merge", compiler_params=SMALL
    )(core, left, right)
    parts = lax.all_to_all(parts, "offset", 0, 0)
    adjoint = pl.pallas_call(
        total_kernel, out_shape=shape((depth, rows, cols), f32), name="total", compiler_params=SMALL
    )(parts)
    return image, adjoint


def solution(mesh):
    field = P(None, "offset", "space")
    in_specs = (field,) * 5 + (P("offset", None), P("offset", None, None, "space"))
    out_specs = (P("offset", None, None, "space"), field)
    return jax.shard_map(
        on_device, mesh=mesh, in_specs=in_specs, out_specs=out_specs, check_vma=False
    )
```

```python
import functools

import jax
import jax.numpy as jnp
from jax import lax
from jax.experimental import pallas as pl
from jax.experimental.pallas import tpu as pltpu
from jax.sharding import PartitionSpec as P

OFF_SIDE = 16
HMAX = 8
STEPS = 2
REACH = HMAX + STEPS
LANES = 128
UNROLL = 2
SMALL = pltpu.CompilerParams(vmem_limit_bytes=6 * 2**20)

CALLS = (
    ((7, 16, 16), (0, 0, 32), (1, 0, 16)),
    ((1, 16, 16), (2, 0, 16), (6, 16, 16), (7, 0, 16)),
    ((2, 16, 16), (3, 0, 16), (5, 16, 16), (6, 0, 16)),
    ((3, 16, 16), (4, 0, 32), (5, 0, 16)),
)


def swaps(count):
    inner = [(i, i ^ 1) for i in range(count)]
    outer = [(i, i + 1 if i % 2 else i - 1) for i in range(1, count - 1)]
    return inner, outer


def roll_lanes(x, shift):
    return pltpu.roll(x, shift % LANES, x.ndim - 1)


def edges_kernel(*refs):
    fields, raw_ref, edge_ref = refs[:-2], refs[-2], refs[-1]
    depth, rows, cols = fields[0].shape
    total = len(fields) * rows
    lane = lax.broadcasted_iota(jnp.int32, (total, LANES), 1)
    packed = jnp.zeros((total, LANES), jnp.float32)
    for z in range(depth):
        plane = jnp.concatenate([ref[z] for ref in fields], axis=0)
        for f in range(len(fields)):
            raw_ref[f, z] = plane[f * rows:(f + 1) * rows]
        first = roll_lanes(plane, 32 * z)
        last = roll_lanes(plane, 32 * z + 32)
        packed = jnp.where((lane >= 32 * z) & (lane < 32 * z + 16), first, packed)
        packed = jnp.where((lane >= 32 * z + 16) & (lane < 32 * z + 32), last, packed)
    for f in range(len(fields)):
        edge_ref[f] = packed[f * rows:(f + 1) * rows]


def touch_kernel(ref, out_ref):
    out_ref[...] = ref[0, 0, :8, :].astype(jnp.float32)


def widen_kernel(where_ref, shifts_ref, raw_ref, inner_ref, outer_ref, wide_ref, send_in_ref, send_out_ref):
    fields, depth, rows, cols = raw_ref.shape
    total = fields * rows
    lane = lax.broadcasted_iota(jnp.int32, (total, LANES), 1)
    row = lax.broadcasted_iota(jnp.int32, (8, 2 * LANES), 0)
    even_x = where_ref[1] == 0
    even_y = where_ref[2] == 0
    inner = jnp.concatenate([inner_ref[f] for f in range(fields)], axis=0)
    outer = jnp.concatenate([outer_ref[f] for f in range(fields)], axis=0)
    left = jnp.where(even_x, outer, inner)
    right = jnp.where(even_x, inner, outer)
    upper = [jnp.zeros((8, 2 * LANES), jnp.float32) for _ in range(fields)]
    lower = list(upper)
    for z in range(depth):
        beside = jnp.where(lane >= cols - REACH, roll_lanes(left, 96 - 32 * z), 0.0)
        beside = jnp.where(lane < REACH, roll_lanes(right, -32 * z), beside)
        here = (row >= 2 * z) & (row < 2 * z + 2)
        for f in range(fields):
            both = jnp.concatenate([raw_ref[f, z], beside[f * rows:(f + 1) * rows]], axis=1)
            wide_ref[f, z] = both
            upper[f] = jnp.where(here, pltpu.roll(both[:8], 2 * z, 0), upper[f])
            lower[f] = jnp.where(here, pltpu.roll(both[rows - 8:], (2 * z + 2) % 8, 0), lower[f])
    for f in range(fields):
        send_in_ref[f] = jnp.where(even_y, lower[f], upper[f])
        send_out_ref[f] = jnp.where(even_y, upper[f], lower[f])


def wave_kernel(where_ref, wide_ref, inner_ref, outer_ref, tile_ref):
    depth, rows, width = wide_ref.shape[1:]
    high_rows = rows + 8
    lane = lax.broadcasted_iota(jnp.int32, (rows, LANES), 1)
    edge_row = lax.broadcasted_iota(jnp.int32, (8, width), 0)
    even_y = where_ref[2] == 0
    top = [jnp.where(even_y, outer_ref[f], inner_ref[f]) for f in range(5)]
    bottom = [jnp.where(even_y, inner_ref[f], outer_ref[f]) for f in range(5)]

    def whole(f, z):
        edge = jnp.where(edge_row >= 6, pltpu.roll(top[f], (6 - 2 * z) % 8, 0), 0.0)
        edge = jnp.where(edge_row < 2, pltpu.roll(bottom[f], (8 - 2 * z) % 8, 0), edge)
        return jnp.concatenate([wide_ref[f, z], edge], axis=0)

    speed = [whole(4, z) for z in range(depth)]

    def advance(prev, now):
        out = []
        for z in range(depth):
            c = now[z]
            beside = pltpu.roll(c, 1, 0) + pltpu.roll(c, high_rows - 1, 0)
            beside = beside + pltpu.roll(c, 1, 1) + pltpu.roll(c, width - 1, 1)
            if z > 0:
                beside = beside + now[z - 1]
            if z < depth - 1:
                beside = beside + now[z + 1]
            out.append(2.0 * c - prev[z] + speed[z] * (beside - 6.0 * c))
        return out

    packed = [jnp.zeros((rows, LANES), jnp.float32) for _ in range(2)]
    for pair in range(2):
        prev = [whole(2 * pair, z) for z in range(depth)]
        now = [whole(2 * pair + 1, z) for z in range(depth)]
        for t in range(STEPS):
            prev, now = now, advance(prev, now)
            for z in range(depth):
                plane = (pair * STEPS + t) * depth + z
                tile_ref[plane] = now[z][:rows, :LANES]
                q = plane % 8
                beside = roll_lanes(now[z][:rows, LANES:], (8 + 16 * q) % LANES)
                here = (lane >= 16 * q) & (lane < 16 * q + 16)
                packed[plane // 8] = jnp.where(here, beside, packed[plane // 8])
    for k in range(2):
        tile_ref[4 * depth + k] = packed[k]


def needed(call):
    return sorted({r for r, _, _ in call} | {(r + k) % 8 for r, a, m in call for k in (-1, 1)
                   if (k < 0 and a == 0) or (k > 0 and a + m == 32)})


def image_kernel(call, first, last, *refs):
    refs = list(refs)
    where_ref, shifts_ref, observed_ref = refs[:3]
    del refs[:4 if first else 3]
    tiles = {}
    for r in needed(call):
        tiles[r], refs = refs[:2], refs[2:]
    if not first:
        refs = refs[1:]
    segments = list(call)
    earlier = []
    if last:
        for other in CALLS:
            if other != call:
                for segment in other:
                    earlier.append((segment, refs[0], refs[1]))
                    refs = refs[2:]
    n_seg = len(segments)
    image_hbm, refs = refs[0], refs[1:]
    if last:
        core_out, send_in, send_out = refs[:3]
        refs = refs[3:]
    sums = []
    for _ in segments:
        sums.append(refs[:2])
        refs = refs[2:]
    mains, sides, images = refs[:n_seg], refs[n_seg:2 * n_seg], refs[2 * n_seg:3 * n_seg]
    sems = refs[3 * n_seg]
    count, depth, all_rows = observed_ref.shape[:3]
    planes = 4 * depth
    rows = all_rows // 8
    half = rows // 2

    def z_of(r):
        return lax.rem(where_ref[0] + r, 8)

    def put(n, part):
        r, a, m = segments[n]
        at = pl.multiple_of(z_of(r) * rows + a, half)
        which = pl.ds(part * (count // 2), count // 2)
        return pltpu.make_async_copy(
            images[n].at[which], image_hbm.at[which, :, pl.ds(at, m), :], sems.at[n, part]
        )

    packs, homes = [], []
    for n, (r, a, m) in enumerate(segments):
        for ref in sums[n]:
            ref[...] = jnp.zeros_like(ref)
        for b in range(a - HMAX, a + m + HMAX, 8):
            step = -1 if b < 0 else (1 if b >= rows else 0)
            b_in = b - step * rows
            ref = tiles[(r + step) % 8][b_in // half]
            part = slice(b_in % half, b_in % half + 8)
            inside = {-1: z_of(r) > 0, 0: None, 1: z_of(r) < 7}[step]
            to = slice(b - a + HMAX, b - a + HMAX + 8)

            def load(p):
                value = ref[p, part, :]
                return value if inside is None else jnp.where(inside, value, 0.0)

            for p in range(planes):
                mains[n][p, to, :] = load(p)
            for k in range(2):
                packs.append(load(planes + k))
                homes.append((n, 8 * k, to))
    packs = jnp.concatenate(packs, axis=0)
    for q in range(8):
        turned = roll_lanes(packs, -(8 + 16 * q))
        for i, (n, p, to) in enumerate(homes):
            sides[n][p + q, to, :] = turned[8 * i:8 * i + 8]

    lane = lax.broadcasted_iota(jnp.int32, (rows, LANES), 1)

    def rotated(pieces, amount):
        turned = pltpu.roll(jnp.concatenate(pieces, axis=0), amount, 1)
        out, at = [], 0
        for x in pieces:
            out.append(turned[at:at + x.shape[0]])
            at += x.shape[0]
        return out

    def per_offset(o, carry):
        hx = shifts_ref[o, 0]
        hy = shifts_ref[o, 1]
        wrap_s = (lane < -hx) | (lane >= LANES - hx)
        wrap_r = (lane < hx) | (lane >= LANES + hx)
        to_s = lax.rem(hx + LANES, LANES)
        to_r = lax.rem(LANES - hx, LANES)
        s_at = HMAX - hy
        r_at = HMAX + hy

        def piece(n, plane, start, wrap):
            m = segments[n][2]
            a = mains[n][plane, pl.ds(start, m), :]
            return jnp.where(wrap[:m], sides[n][plane, pl.ds(start, m), :], a)

        parts = [(n, z) for n in range(n_seg) for z in range(depth)]
        sources, receivers = [], []
        for n, z in parts:
            for t in range(STEPS):
                sources.append(piece(n, t * depth + z, s_at, wrap_s))
                receivers.append(piece(n, (STEPS + t) * depth + z, r_at, wrap_r))
        sources = rotated(sources, to_s)
        receivers = rotated(receivers, to_r)
        terms = []
        for i, (n, z) in enumerate(parts):
            r, a, m = segments[n]
            s1, s2 = sources[2 * i:2 * i + 2]
            r1, r2 = receivers[2 * i:2 * i + 2]
            full = s1 * r1 + s2 * r2
            images[n][o, z] = full.astype(jnp.bfloat16)
            y_at = pl.multiple_of(z_of(r) * rows + a, half)
            observed = observed_ref[o, z, pl.ds(y_at, m), :].astype(jnp.float32)
            terms.append((full - observed) * s2)
        terms = rotated(terms, to_s)
        kept = []
        for (n, z), t in zip(parts, terms):
            m = segments[n][2]
            at = (z, pl.ds(r_at, m))
            inner = sums[n][0][at] + jnp.where(wrap_r[:m], 0.0, t)
            outer = sums[n][1][at] + jnp.where(wrap_r[:m], t, 0.0)
            kept.append((n, at, inner, outer))
        for n, at, inner, outer in kept:
            sums[n][0][at] = inner
            sums[n][1][at] = outer
        return carry

    for part in range(2):
        lax.fori_loop(part * (count // 2), (part + 1) * (count // 2), per_offset, 0, unroll=UNROLL)
        for n in range(n_seg):
            put(n, part).start()

    if last:
        all_core, all_side = refs[3 * n_seg + 1:]
        all_core[...] = jnp.zeros_like(all_core)
        all_side[...] = jnp.zeros_like(all_side)
        mine = [(segment, c, e) for segment, (c, e) in zip(segments, sums)]
        for (r, a, m), c, e in earlier + mine:
            at = pl.multiple_of(z_of(r) * rows + a, half)
            all_core[:, pl.ds(at, m + 2 * HMAX), :] += c[...]
            all_side[:, pl.ds(at, m + 2 * HMAX), :] += e[...]
        n_tiles = all_rows // half
        for tile in range(n_tiles):
            at = HMAX + tile * half
            for z in range(depth):
                core_out[tile, z * half:(z + 1) * half, :] = all_core[z, at:at + half, :]
        lane8 = lax.broadcasted_iota(jnp.int32, (8 * n_tiles, LANES), 1)
        strip = jnp.zeros((8 * n_tiles, LANES), jnp.float32)
        for q in range(8):
            z, k = q % 4, q // 4
            starts = [HMAX + tile * half + 8 * k for tile in range(n_tiles)]
            part = jnp.concatenate([all_side[z, at:at + 8, :] for at in starts], axis=0)
            here = (lane8 >= 16 * q) & (lane8 < 16 * q + 16)
            strip = jnp.where(here, roll_lanes(part, 8 + 16 * q), strip)
        cut = 4 * n_tiles
        low = lax.rem(lane8[:cut], 16) < HMAX
        lefts = jnp.where(low, strip[:cut], roll_lanes(strip[cut:], HMAX))
        rights = jnp.where(low, roll_lanes(strip[:cut], -HMAX), strip[cut:])
        even_x = where_ref[1] == 0
        send_in[...] = jnp.where(even_x, rights, lefts)
        send_out[...] = jnp.where(even_x, lefts, rights)
    for n in range(n_seg):
        for part in range(2):
            put(n, part).wait()


def merge_kernel(where_ref, core_ref, inner_ref, outer_ref, out_ref):
    n_tiles = core_ref.shape[0]
    cut = inner_ref.shape[0]
    even_x = where_ref[1] == 0
    from_right = jnp.where(even_x, inner_ref[...], outer_ref[...])
    from_left = jnp.where(even_x, outer_ref[...], inner_ref[...])
    lane = lax.broadcasted_iota(jnp.int32, (cut, LANES), 1)
    for group in range(2):
        for q in range(8):
            slot = 16 * q + HMAX * group
            extra = jnp.where(lane < HMAX, roll_lanes(from_left, -slot), 0.0)
            extra = jnp.where(lane >= LANES - HMAX, roll_lanes(from_right, 120 - slot), extra)
            at = (q % 4) * 16 + (q // 4) * 8
            for i in range(n_tiles // 2):
                tile = group * (n_tiles // 2) + i
                out_ref[tile, at:at + 8, :] = core_ref[tile, at:at + 8, :] + extra[8 * i:8 * i + 8]


def total_kernel(parts_ref, out_ref):
    total = parts_ref[0]
    for i in range(1, parts_ref.shape[0]):
        total = total + parts_ref[i]
    rows = out_ref.shape[1]
    for z in range(out_ref.shape[0]):
        out_ref[z] = total[z * rows:(z + 1) * rows] * (1.0 / OFF_SIDE)


def on_device(src_prev, src_now, rcv_prev, rcv_now, velocity, shift_table, ref_image):
    depth, rows, cols = src_now.shape
    n_off = lax.axis_size("offset")
    n_space = lax.axis_size("space")
    all_rows = ref_image.shape[2]
    shape = jax.ShapeDtypeStruct
    f32 = jnp.float32
    whole = pl.BlockSpec(memory_space=pltpu.VMEM)
    scalars = pl.BlockSpec(memory_space=pltpu.SMEM)
    anywhere = pl.BlockSpec(memory_space=pl.ANY)
    me = lax.axis_index("offset")
    where = jnp.stack([me // 2, lax.axis_index("space") % 2, me % 2]).astype(jnp.int32)

    raw, edge = pl.pallas_call(
        edges_kernel,
        out_shape=[shape((5, depth, rows, cols), f32), shape((5, rows, cols), f32)],
        name="edges",
    )(src_prev, src_now, rcv_prev, rcv_now, velocity)
    inner_x, outer_x = swaps(n_space)
    inner_y, outer_y = swaps(n_off)
    got_in = lax.ppermute(edge, "space", inner_x)
    got_out = lax.ppermute(edge, "space", outer_x)
    line = shape((5, 8, 2 * LANES), f32)
    wide, send_in, send_out = pl.pallas_call(
        widen_kernel,
        in_specs=[scalars] * 2 + [whole] * 3,
        out_shape=[shape((5, depth, rows, 2 * LANES), f32), line, line],
        name="widen", compiler_params=SMALL,
    )(where, shift_table, raw, got_in, got_out)
    got_in = lax.ppermute(send_in, "offset", inner_y)
    got_out = lax.ppermute(send_out, "offset", outer_y)
    planes = 4 * depth + 2
    tile = pl.pallas_call(
        wave_kernel,
        in_specs=[scalars] + [whole] * 3,
        out_shape=shape((planes, rows, LANES), f32),
        name="wave", compiler_params=SMALL,
    )(where, wide, got_in, got_out)

    other = lax.ppermute(tile, "offset", inner_y)
    is_low = (me % 2) == 0
    pair = jnp.stack([jnp.where(is_low, tile, other), jnp.where(is_low, other, tile)])

    def turn(d):
        return [(i, (i - 2 * d) % n_off) for i in range(n_off)]

    tiles = [(pair[0], pair[1])] + [None] * 7
    touched = pl.pallas_call(
        touch_kernel,
        in_specs=[whole],
        out_specs=whole,
        out_shape=shape((8, LANES), f32),
        compiler_params=SMALL,
        cost_estimate=pl.CostEstimate(flops=0, bytes_accessed=8_000_000, transcendentals=0),
        name="touch",
    )(ref_image)
    local = shift_table.shape[0]
    image = None
    done = []
    up = down = pair
    for at, call in enumerate(CALLS):
        first, last = call == CALLS[0], call == CALLS[-1]
        if first:
            up = lax.ppermute(pair, "offset", turn(1))
            down = lax.ppermute(pair, "offset", turn(-1))
            up, down, touched = lax.optimization_barrier((up, down, touched))
            tiles[1], tiles[7] = (up[0], up[1]), (down[0], down[1])
        if at < 2:
            next_up = lax.ppermute(up, "offset", turn(1))
            next_down = lax.ppermute(down, "offset", turn(-1))
        elif at == 2:
            next_up = lax.ppermute(up[0], "offset", turn(1))
            next_down = lax.ppermute(down[1], "offset", turn(-1))
        args = [where, shift_table, ref_image]
        specs = [scalars, scalars, whole]
        if first:
            args.append(touched)
            specs.append(whole)
        for r in needed(call):
            args += tiles[r]
            specs += [whole, whole]
        aliases = {}
        if not first:
            aliases = {len(args): 0}
            args.append(image)
            specs.append(anywhere)
        sums = [(depth, m + 2 * HMAX, LANES) for _, _, m in call for _ in range(2)]
        fields = [pltpu.VMEM((4 * depth, m + 2 * HMAX, LANES), f32) for _, _, m in call]
        scratch = fields + fields
        scratch += [pltpu.VMEM((local, depth, m, LANES), jnp.bfloat16) for _, _, m in call]
        scratch += [pltpu.SemaphoreType.DMA((len(call), 2))]
        if last:
            args += done
            specs += [whole] * len(done)
            scratch = [pltpu.VMEM(dims, f32) for dims in sums] + scratch
            scratch += [pltpu.VMEM((depth, all_rows + 2 * HMAX, LANES), f32)] * 2
            half_strip = shape((n_off * 4, LANES), f32)
            outs = [shape((n_off, depth * rows, LANES), f32), half_strip, half_strip]
        else:
            outs = [shape(dims, f32) for dims in sums]
        image, *rest = pl.pallas_call(
            functools.partial(image_kernel, call, first, last),
            in_specs=specs,
            out_specs=[anywhere] + [whole] * len(outs),
            out_shape=[shape(ref_image.shape, jnp.bfloat16)] + outs,
            scratch_shapes=scratch,
            input_output_aliases=aliases,
            compiler_params=pltpu.CompilerParams(vmem_limit_bytes=16 * 2**20),
            cost_estimate=pl.CostEstimate(
                flops=20_000_000, bytes_accessed=8_000_000, transcendentals=0
            ),
            name="image",
        )(*args)
        done += rest
        if not last:
            up, down, image = lax.optimization_barrier((next_up, next_down, image))
            if at < 2:
                tiles[at + 2], tiles[6 - at] = (up[0], up[1]), (down[0], down[1])
            else:
                tiles[4] = (up, down)

    core, send_in, send_out = rest
    got_in = lax.ppermute(send_in, "space", inner_x)
    got_out = lax.ppermute(send_out, "space", outer_x)
    parts = pl.pallas_call(
        merge_kernel,
        in_specs=[scalars] + [whole] * 3,
        out_shape=shape(core.shape, f32),
        name="merge", compiler_params=SMALL,
    )(where, core, got_in, got_out)
    parts = lax.all_to_all(parts, "offset", 0, 0)
    adjoint = pl.pallas_call(
        total_kernel, out_shape=shape((depth, rows, cols), f32), name="total", compiler_params=SMALL
    )(parts)
    return image, adjoint


def solution(mesh):
    field = P(None, "offset", "space")
    in_specs = (field,) * 5 + (P("offset", None), P("offset", None, None, "space"))
    out_specs = (P("offset", None, None, "space"), field)
    return jax.shard_map(
        on_device, mesh=mesh, in_specs=in_specs, out_specs=out_specs, check_vma=False
    )
```

```python
import functools

import jax
import jax.numpy as jnp
from jax import lax
from jax.experimental import pallas as pl
from jax.experimental.pallas import tpu as pltpu
from jax.sharding import PartitionSpec as P

OFF_SIDE = 16
HMAX = 8
STEPS = 2
REACH = HMAX + STEPS
LANES = 128
UNROLL = 2
SMALL = pltpu.CompilerParams(vmem_limit_bytes=6 * 2**20)

CALLS = (
    ((7, 8, 24), (0, 0, 32), (1, 0, 24)),
    ((1, 24, 8), (2, 0, 24), (6, 8, 24), (7, 0, 8)),
    ((2, 24, 8), (3, 0, 24), (5, 8, 24), (6, 0, 8)),
    ((3, 24, 8), (4, 0, 32), (5, 0, 8)),
)


def swaps(count):
    inner = [(i, i ^ 1) for i in range(count)]
    outer = [(i, i + 1 if i % 2 else i - 1) for i in range(1, count - 1)]
    return inner, outer


def whole_tiles(rows):
    return -(-rows // 16) * 16


def roll_lanes(x, shift):
    return pltpu.roll(x, shift % LANES, x.ndim - 1)


def edges_kernel(*refs):
    fields, raw_ref, edge_ref = refs[:-2], refs[-2], refs[-1]
    depth, rows, cols = fields[0].shape
    total = len(fields) * rows
    lane = lax.broadcasted_iota(jnp.int32, (total, LANES), 1)
    packed = jnp.zeros((total, LANES), jnp.float32)
    for z in range(depth):
        plane = jnp.concatenate([ref[z] for ref in fields], axis=0)
        for f in range(len(fields)):
            raw_ref[f, z] = plane[f * rows:(f + 1) * rows]
        first = roll_lanes(plane, 32 * z)
        last = roll_lanes(plane, 32 * z + 32)
        packed = jnp.where((lane >= 32 * z) & (lane < 32 * z + 16), first, packed)
        packed = jnp.where((lane >= 32 * z + 16) & (lane < 32 * z + 32), last, packed)
    for f in range(len(fields)):
        edge_ref[f] = packed[f * rows:(f + 1) * rows]


def hold_kernel(ref, out_ref):
    out_ref[...] = ref[...]


def touch_kernel(ref, out_ref):
    out_ref[...] = ref[0, 0, :8, :].astype(jnp.float32)


def spread(packed, z):
    lane = lax.broadcasted_iota(jnp.int32, packed.shape, 1)
    beside = jnp.where(lane >= LANES - REACH, roll_lanes(packed, 96 - 32 * z), 0.0)
    return jnp.where(lane < REACH, roll_lanes(packed, -32 * z), beside)


def widen_kernel(where_ref, shifts_ref, raw_ref, inner_ref, outer_ref, own_ref, line_ref):
    fields, depth, rows, cols = raw_ref.shape
    lane = lax.broadcasted_iota(jnp.int32, (fields * rows, LANES), 1)
    row = lax.broadcasted_iota(jnp.int32, (8, 2 * LANES), 0)
    even_x = where_ref[1] == 0
    even_y = where_ref[2] == 0
    inner = jnp.concatenate([inner_ref[f] for f in range(fields)], axis=0)
    outer = jnp.concatenate([outer_ref[f] for f in range(fields)], axis=0)
    left = jnp.where(even_x, outer, inner)
    right = jnp.where(even_x, inner, outer)
    packed = jnp.where(lax.rem(lane, 32) < 16, right, left)
    for f in range(fields):
        own_ref[fields * depth + f] = packed[f * rows:(f + 1) * rows]
        for z in range(depth):
            own_ref[f * depth + z] = raw_ref[f, z]
    lines = [jnp.zeros((8, 2 * LANES), jnp.float32) for _ in range(fields)]
    for z in range(depth):
        beside = spread(packed, z)
        here = (row >= 2 * z) & (row < 2 * z + 2)
        for f in range(fields):
            both = jnp.concatenate([raw_ref[f, z], beside[f * rows:(f + 1) * rows]], axis=1)
            upper = pltpu.roll(both[:8], 2 * z, 0)
            lower = pltpu.roll(both[rows - 8:], (2 * z + 2) % 8, 0)
            lines[f] = jnp.where(here, jnp.where(even_y, upper, lower), lines[f])
    for f in range(fields):
        line_ref[f] = lines[f]


def wave_kernel(where_ref, own_ref, other_ref, near_ref, far_ref, pair_ref):
    fields = near_ref.shape[0]
    depth = own_ref.shape[0] // fields - 1
    half = own_ref.shape[1]
    rows = 2 * half
    width = 2 * LANES
    high_rows = rows + 8
    lane = lax.broadcasted_iota(jnp.int32, (rows, LANES), 1)
    edge_row = lax.broadcasted_iota(jnp.int32, (8, width), 0)
    even_y = where_ref[2] == 0

    def ordered(mine, other):
        return [jnp.where(even_y, mine, other), jnp.where(even_y, other, mine)]

    packed_all = []
    for f in range(fields):
        packed_all += ordered(own_ref[fields * depth + f], other_ref[fields * depth + f])
    packed_all = jnp.concatenate(packed_all, axis=0)
    besides = [spread(packed_all, z) for z in range(depth)]
    top = [jnp.where(even_y, near_ref[f], far_ref[f]) for f in range(fields)]
    bottom = [jnp.where(even_y, far_ref[f], near_ref[f]) for f in range(fields)]

    def whole(f, z):
        edge = jnp.where(edge_row >= 6, pltpu.roll(top[f], (6 - 2 * z) % 8, 0), 0.0)
        edge = jnp.where(edge_row < 2, pltpu.roll(bottom[f], (8 - 2 * z) % 8, 0), edge)
        plane = f * depth + z
        body = jnp.concatenate(ordered(own_ref[plane], other_ref[plane]), axis=0)
        beside = besides[z][f * rows:(f + 1) * rows]
        both = jnp.concatenate([body, beside], axis=1)
        return jnp.concatenate([both, edge], axis=0)

    speed = [whole(4, z) for z in range(depth)]

    def advance(prev, now):
        out = []
        for z in range(depth):
            c = now[z]
            near = pltpu.roll(c, 1, 0) + pltpu.roll(c, high_rows - 1, 0)
            near = near + pltpu.roll(c, 1, 1) + pltpu.roll(c, width - 1, 1)
            if z > 0:
                near = near + now[z - 1]
            if z < depth - 1:
                near = near + now[z + 1]
            out.append(2.0 * c - prev[z] + speed[z] * (near - 6.0 * c))
        return out

    packed = [jnp.zeros((rows, LANES), jnp.float32) for _ in range(2)]
    for pair in range(2):
        prev = [whole(2 * pair, z) for z in range(depth)]
        now = [whole(2 * pair + 1, z) for z in range(depth)]
        for t in range(STEPS):
            prev, now = now, advance(prev, now)
            for z in range(depth):
                plane = (pair * STEPS + t) * depth + z
                q = plane % 8
                for k in range(2):
                    pair_ref[k, plane] = now[z][k * half:(k + 1) * half, :LANES]
                beside = roll_lanes(now[z][:rows, LANES:], 8 + 16 * q)
                here = (lane >= 16 * q) & (lane < 16 * q + 16)
                packed[plane // 8] = jnp.where(here, beside, packed[plane // 8])
    for j in range(2):
        for k in range(2):
            pair_ref[k, 4 * depth + j] = packed[j][k * half:(k + 1) * half]


def needed(call):
    return sorted({r for r, _, _ in call} | {(r + k) % 8 for r, a, m in call for k in (-1, 1)
                   if (k < 0 and a == 0) or (k > 0 and a + m == 32)})


def image_kernel(call, first, last, *refs):
    refs = list(refs)
    where_ref, shifts_ref, observed_ref = refs[:3]
    del refs[:4 if first else 3]
    tiles = {}
    for r in needed(call):
        tiles[r], refs = refs[:2], refs[2:]
    if not first:
        refs = refs[1:]
    segments = list(call)
    earlier = []
    if last:
        for other in CALLS:
            if other != call:
                for segment in other:
                    earlier.append((segment, refs[0], refs[1]))
                    refs = refs[2:]
    n_seg = len(segments)
    image_hbm, refs = refs[0], refs[1:]
    if last:
        core_out, send_in, send_out = refs[:3]
        refs = refs[3:]
    sums = []
    for _ in segments:
        sums.append(refs[:2])
        refs = refs[2:]
    mains, sides, images = refs[:n_seg], refs[n_seg:2 * n_seg], refs[2 * n_seg:3 * n_seg]
    sems = refs[3 * n_seg]
    count, depth, all_rows = observed_ref.shape[:3]
    planes = 4 * depth
    rows = all_rows // 8
    half = rows // 2

    def z_of(r):
        return lax.rem(where_ref[0] + r, 8)

    def put(n, part):
        r, a, m = segments[n]
        at = pl.multiple_of(z_of(r) * rows + a, 8)
        which = pl.ds(part * (count // 2), count // 2)
        return pltpu.make_async_copy(
            images[n].at[which, :, pl.ds(0, m), :],
            image_hbm.at[which, :, pl.ds(at, m), :],
            sems.at[n, part],
        )

    packs, homes = [], []
    for n, (r, a, m) in enumerate(segments):
        for ref in sums[n]:
            ref[...] = jnp.zeros_like(ref)
        for b in range(a - HMAX, a + m + HMAX, 8):
            step = -1 if b < 0 else (1 if b >= rows else 0)
            b_in = b - step * rows
            ref = tiles[(r + step) % 8][b_in // half]
            part = slice(b_in % half, b_in % half + 8)
            inside = {-1: z_of(r) > 0, 0: None, 1: z_of(r) < 7}[step]
            to = slice(b - a + HMAX, b - a + HMAX + 8)

            def load(p):
                value = ref[p, part, :]
                return value if inside is None else jnp.where(inside, value, 0.0)

            for p in range(planes):
                mains[n][p, to, :] = load(p)
            for k in range(2):
                packs.append(load(planes + k))
                homes.append((n, 8 * k, to))
    packs = jnp.concatenate(packs, axis=0)
    for q in range(8):
        turned = roll_lanes(packs, -(8 + 16 * q))
        for i, (n, p, to) in enumerate(homes):
            sides[n][p + q, to, :] = turned[8 * i:8 * i + 8]

    lane = lax.broadcasted_iota(jnp.int32, (rows, LANES), 1)

    def rotated(pieces, amount):
        turned = pltpu.roll(jnp.concatenate(pieces, axis=0), amount, 1)
        out, at = [], 0
        for x in pieces:
            out.append(turned[at:at + x.shape[0]])
            at += x.shape[0]
        return out

    def per_offset(o, carry):
        hx = shifts_ref[o, 0]
        hy = shifts_ref[o, 1]
        wrap_s = (lane < -hx) | (lane >= LANES - hx)
        wrap_r = (lane < hx) | (lane >= LANES + hx)
        to_s = lax.rem(hx + LANES, LANES)
        to_r = lax.rem(LANES - hx, LANES)
        s_at = HMAX - hy
        r_at = HMAX + hy

        def piece(n, plane, start, wrap):
            m = segments[n][2]
            a = mains[n][plane, pl.ds(start, m), :]
            return jnp.where(wrap[:m], sides[n][plane, pl.ds(start, m), :], a)

        parts = [(n, z) for n in range(n_seg) for z in range(depth)]
        sources, receivers = [], []
        for n, z in parts:
            for t in range(STEPS):
                sources.append(piece(n, t * depth + z, s_at, wrap_s))
                receivers.append(piece(n, (STEPS + t) * depth + z, r_at, wrap_r))
        sources = rotated(sources, to_s)
        receivers = rotated(receivers, to_r)
        terms = []
        for i, (n, z) in enumerate(parts):
            r, a, m = segments[n]
            s1, s2 = sources[2 * i:2 * i + 2]
            r1, r2 = receivers[2 * i:2 * i + 2]
            full = s1 * r1 + s2 * r2
            images[n][o, z, :m] = full.astype(jnp.bfloat16)
            lead = a % half
            y_at = pl.multiple_of(z_of(r) * rows + a - lead, half)
            observed = observed_ref[o, z, pl.ds(y_at, whole_tiles(lead + m)), :]
            observed = observed.astype(jnp.float32)[lead:lead + m]
            terms.append((full - observed) * s2)
        terms = rotated(terms, to_s)
        kept = []
        for (n, z), t in zip(parts, terms):
            m = segments[n][2]
            at = (z, pl.ds(r_at, m))
            inner = sums[n][0][at] + jnp.where(wrap_r[:m], 0.0, t)
            outer = sums[n][1][at] + jnp.where(wrap_r[:m], t, 0.0)
            kept.append((n, at, inner, outer))
        for n, at, inner, outer in kept:
            sums[n][0][at] = inner
            sums[n][1][at] = outer
        return carry

    for part in range(2):
        lax.fori_loop(part * (count // 2), (part + 1) * (count // 2), per_offset, 0, unroll=UNROLL)
        for n in range(n_seg):
            put(n, part).start()

    if last:
        all_core, all_side = refs[3 * n_seg + 1:]
        all_core[...] = jnp.zeros_like(all_core)
        all_side[...] = jnp.zeros_like(all_side)
        mine = [(segment, c, e) for segment, (c, e) in zip(segments, sums)]
        for (r, a, m), c, e in earlier + mine:
            at = pl.multiple_of(z_of(r) * rows + a, 8)
            all_core[:, pl.ds(at, m + 2 * HMAX), :] += c[...]
            all_side[:, pl.ds(at, m + 2 * HMAX), :] += e[...]
        n_tiles = all_rows // half
        for tile in range(n_tiles):
            at = HMAX + tile * half
            for z in range(depth):
                core_out[tile, z * half:(z + 1) * half, :] = all_core[z, at:at + half, :]
        lane8 = lax.broadcasted_iota(jnp.int32, (8 * n_tiles, LANES), 1)
        strip = jnp.zeros((8 * n_tiles, LANES), jnp.float32)
        for q in range(8):
            z, k = q % 4, q // 4
            starts = [HMAX + tile * half + 8 * k for tile in range(n_tiles)]
            part = jnp.concatenate([all_side[z, at:at + 8, :] for at in starts], axis=0)
            here = (lane8 >= 16 * q) & (lane8 < 16 * q + 16)
            strip = jnp.where(here, roll_lanes(part, 8 + 16 * q), strip)
        cut = 4 * n_tiles
        low = lax.rem(lane8[:cut], 16) < HMAX
        lefts = jnp.where(low, strip[:cut], roll_lanes(strip[cut:], HMAX))
        rights = jnp.where(low, roll_lanes(strip[:cut], -HMAX), strip[cut:])
        even_x = where_ref[1] == 0
        send_in[...] = jnp.where(even_x, rights, lefts)
        send_out[...] = jnp.where(even_x, lefts, rights)
    for n in range(n_seg):
        for part in range(2):
            put(n, part).wait()


def merge_kernel(where_ref, core_ref, inner_ref, outer_ref, out_ref):
    n_tiles = core_ref.shape[0]
    cut = inner_ref.shape[0]
    even_x = where_ref[1] == 0
    from_right = jnp.where(even_x, inner_ref[...], outer_ref[...])
    from_left = jnp.where(even_x, outer_ref[...], inner_ref[...])
    lane = lax.broadcasted_iota(jnp.int32, (cut, LANES), 1)
    for group in range(2):
        for q in range(8):
            slot = 16 * q + HMAX * group
            extra = jnp.where(lane < HMAX, roll_lanes(from_left, -slot), 0.0)
            extra = jnp.where(lane >= LANES - HMAX, roll_lanes(from_right, 120 - slot), extra)
            at = (q % 4) * 16 + (q // 4) * 8
            for i in range(n_tiles // 2):
                tile = group * (n_tiles // 2) + i
                out_ref[tile, at:at + 8, :] = core_ref[tile, at:at + 8, :] + extra[8 * i:8 * i + 8]


def total_kernel(parts_ref, out_ref):
    total = parts_ref[0]
    for i in range(1, parts_ref.shape[0]):
        total = total + parts_ref[i]
    rows = out_ref.shape[1]
    for z in range(out_ref.shape[0]):
        out_ref[z] = total[z * rows:(z + 1) * rows] * (1.0 / OFF_SIDE)


def on_device(src_prev, src_now, rcv_prev, rcv_now, velocity, shift_table, ref_image):
    depth, rows, cols = src_now.shape
    n_off = lax.axis_size("offset")
    n_space = lax.axis_size("space")
    all_rows = ref_image.shape[2]
    shape = jax.ShapeDtypeStruct
    f32 = jnp.float32
    whole = pl.BlockSpec(memory_space=pltpu.VMEM)
    scalars = pl.BlockSpec(memory_space=pltpu.SMEM)
    anywhere = pl.BlockSpec(memory_space=pl.ANY)
    me = lax.axis_index("offset")
    where = jnp.stack([me // 2, lax.axis_index("space") % 2, me % 2]).astype(jnp.int32)

    raw, edge = pl.pallas_call(
        edges_kernel,
        out_shape=[shape((5, depth, rows, cols), f32), shape((5, rows, cols), f32)],
        name="edges",
    )(src_prev, src_now, rcv_prev, rcv_now, velocity)
    inner_x, outer_x = swaps(n_space)
    inner_y, outer_y = swaps(n_off)
    same_y = [(i, i + 2 if i % 2 else i - 2) for i in range(n_off)]
    same_y = [(i, j) for i, j in same_y if 0 <= j < n_off]
    got_in = lax.ppermute(edge, "space", inner_x)
    got_out = lax.ppermute(edge, "space", outer_x)
    raw = pl.pallas_call(
        hold_kernel,
        in_specs=[whole],
        out_specs=whole,
        out_shape=shape(raw.shape, f32),
        compiler_params=SMALL,
        cost_estimate=pl.CostEstimate(flops=0, bytes_accessed=4_000_000, transcendentals=0),
        name="hold",
    )(raw)
    own, line = pl.pallas_call(
        widen_kernel,
        in_specs=[scalars] * 2 + [whole] * 3,
        out_shape=[shape((5 * depth + 5, rows, cols), f32), shape((5, 8, 2 * LANES), f32)],
        name="widen", compiler_params=SMALL,
    )(where, shift_table, raw, got_in, got_out)
    other = lax.ppermute(own, "offset", inner_y)
    near = lax.ppermute(line, "offset", outer_y)
    far = lax.ppermute(line, "offset", same_y)
    planes = 4 * depth + 2
    pair = pl.pallas_call(
        wave_kernel,
        in_specs=[scalars] + [whole] * 4,
        out_shape=shape((2, planes, rows, LANES), f32),
        name="wave", compiler_params=SMALL,
    )(where, own, other, near, far)

    def turn(d):
        return [(i, (i - 2 * d) % n_off) for i in range(n_off)]

    tiles = [(pair[0], pair[1])] + [None] * 7
    touched = pl.pallas_call(
        touch_kernel,
        in_specs=[whole],
        out_specs=whole,
        out_shape=shape((8, LANES), f32),
        compiler_params=SMALL,
        cost_estimate=pl.CostEstimate(flops=0, bytes_accessed=8_000_000, transcendentals=0),
        name="touch",
    )(ref_image)
    local = shift_table.shape[0]
    image = None
    done = []
    up = down = pair
    for at, call in enumerate(CALLS):
        first, last = call == CALLS[0], call == CALLS[-1]
        if first:
            up = lax.ppermute(pair, "offset", turn(1))
            down = lax.ppermute(pair, "offset", turn(-1))
            up, down, touched = lax.optimization_barrier((up, down, touched))
            tiles[1], tiles[7] = (up[0], up[1]), (down[0], down[1])
        if at < 2:
            next_up = lax.ppermute(up, "offset", turn(1))
            next_down = lax.ppermute(down, "offset", turn(-1))
        elif at == 2:
            next_up = lax.ppermute(up[0], "offset", turn(1))
            next_down = lax.ppermute(down[1], "offset", turn(-1))
        args = [where, shift_table, ref_image]
        specs = [scalars, scalars, whole]
        if first:
            args.append(touched)
            specs.append(whole)
        for r in needed(call):
            args += tiles[r]
            specs += [whole, whole]
        aliases = {}
        if not first:
            aliases = {len(args): 0}
            args.append(image)
            specs.append(anywhere)
        sums = [(depth, m + 2 * HMAX, LANES) for _, _, m in call for _ in range(2)]
        fields = [pltpu.VMEM((4 * depth, m + 2 * HMAX, LANES), f32) for _, _, m in call]
        scratch = fields + fields
        scratch += [pltpu.VMEM((local, depth, whole_tiles(m), LANES), jnp.bfloat16) for _, _, m in call]
        scratch += [pltpu.SemaphoreType.DMA((len(call), 2))]
        if last:
            args += done
            specs += [whole] * len(done)
            scratch = [pltpu.VMEM(dims, f32) for dims in sums] + scratch
            scratch += [pltpu.VMEM((depth, all_rows + 2 * HMAX, LANES), f32)] * 2
            half_strip = shape((n_off * 4, LANES), f32)
            outs = [shape((n_off, depth * rows, LANES), f32), half_strip, half_strip]
        else:
            outs = [shape(dims, f32) for dims in sums]
        image, *rest = pl.pallas_call(
            functools.partial(image_kernel, call, first, last),
            in_specs=specs,
            out_specs=[anywhere] + [whole] * len(outs),
            out_shape=[shape(ref_image.shape, jnp.bfloat16)] + outs,
            scratch_shapes=scratch,
            input_output_aliases=aliases,
            compiler_params=pltpu.CompilerParams(vmem_limit_bytes=16 * 2**20),
            cost_estimate=pl.CostEstimate(
                flops=20_000_000, bytes_accessed=8_000_000, transcendentals=0
            ),
            name="image",
        )(*args)
        done += rest
        if not last:
            up, down, image = lax.optimization_barrier((next_up, next_down, image))
            if at < 2:
                tiles[at + 2], tiles[6 - at] = (up[0], up[1]), (down[0], down[1])
            else:
                tiles[4] = (up, down)

    core, send_in, send_out = rest
    got_in = lax.ppermute(send_in, "space", inner_x)
    got_out = lax.ppermute(send_out, "space", outer_x)
    parts = pl.pallas_call(
        merge_kernel,
        in_specs=[scalars] + [whole] * 3,
        out_shape=shape(core.shape, f32),
        name="merge", compiler_params=SMALL,
    )(where, core, got_in, got_out)
    parts = lax.all_to_all(parts, "offset", 0, 0)
    adjoint = pl.pallas_call(
        total_kernel, out_shape=shape((depth, rows, cols), f32), name="total", compiler_params=SMALL
    )(parts)
    return image, adjoint


def solution(mesh):
    field = P(None, "offset", "space")
    in_specs = (field,) * 5 + (P("offset", None), P("offset", None, None, "space"))
    out_specs = (P("offset", None, None, "space"), field)
    return jax.shard_map(
        on_device, mesh=mesh, in_specs=in_specs, out_specs=out_specs, check_vma=False
    )
```

```python
import functools

import jax
import jax.numpy as jnp
from jax import lax
from jax.experimental import pallas as pl
from jax.experimental.pallas import tpu as pltpu
from jax.sharding import PartitionSpec as P

OFF_SIDE = 16
HMAX = 8
STEPS = 2
REACH = HMAX + STEPS
LANES = 128
GROUP = 4
SMALL = pltpu.CompilerParams(vmem_limit_bytes=6 * 2**20)

CALLS = (
    ((7, 8, 24), (0, 0, 32), (1, 0, 24)),
    ((1, 24, 8), (2, 0, 24), (6, 8, 24), (7, 0, 8)),
    ((2, 24, 8), (3, 0, 24), (5, 8, 24), (6, 0, 8)),
    ((3, 24, 8), (4, 0, 32), (5, 0, 8)),
)


def swaps(count):
    inner = [(i, i ^ 1) for i in range(count)]
    outer = [(i, i + 1 if i % 2 else i - 1) for i in range(1, count - 1)]
    return inner, outer


def whole_tiles(rows):
    return -(-rows // 16) * 16


def roll_lanes(x, shift):
    return pltpu.roll(x, shift % LANES, x.ndim - 1)


def edges_kernel(*refs):
    fields, raw_ref, edge_ref = refs[:-2], refs[-2], refs[-1]
    depth, rows, cols = fields[0].shape
    total = len(fields) * rows
    lane = lax.broadcasted_iota(jnp.int32, (total, LANES), 1)
    packed = jnp.zeros((total, LANES), jnp.float32)
    for z in range(depth):
        plane = jnp.concatenate([ref[z] for ref in fields], axis=0)
        for f in range(len(fields)):
            raw_ref[f, z] = plane[f * rows:(f + 1) * rows]
        first = roll_lanes(plane, 32 * z)
        last = roll_lanes(plane, 32 * z + 32)
        packed = jnp.where((lane >= 32 * z) & (lane < 32 * z + 16), first, packed)
        packed = jnp.where((lane >= 32 * z + 16) & (lane < 32 * z + 32), last, packed)
    for f in range(len(fields)):
        edge_ref[f] = packed[f * rows:(f + 1) * rows]


def hold_kernel(ref, out_ref):
    out_ref[...] = ref[...]


def touch_kernel(ref, out_ref):
    out_ref[...] = ref[0, 0, :8, :].astype(jnp.float32)


def spread(packed, z):
    lane = lax.broadcasted_iota(jnp.int32, packed.shape, 1)
    beside = jnp.where(lane >= LANES - REACH, roll_lanes(packed, 96 - 32 * z), 0.0)
    return jnp.where(lane < REACH, roll_lanes(packed, -32 * z), beside)


def widen_kernel(where_ref, shifts_ref, raw_ref, inner_ref, outer_ref, own_ref, line_ref):
    fields, depth, rows, cols = raw_ref.shape
    lane = lax.broadcasted_iota(jnp.int32, (fields * rows, LANES), 1)
    row = lax.broadcasted_iota(jnp.int32, (8, 2 * LANES), 0)
    even_x = where_ref[1] == 0
    even_y = where_ref[2] == 0
    inner = jnp.concatenate([inner_ref[f] for f in range(fields)], axis=0)
    outer = jnp.concatenate([outer_ref[f] for f in range(fields)], axis=0)
    left = jnp.where(even_x, outer, inner)
    right = jnp.where(even_x, inner, outer)
    packed = jnp.where(lax.rem(lane, 32) < 16, right, left)
    for f in range(fields):
        own_ref[fields * depth + f] = packed[f * rows:(f + 1) * rows]
        for z in range(depth):
            own_ref[f * depth + z] = raw_ref[f, z]
    lines = [jnp.zeros((8, 2 * LANES), jnp.float32) for _ in range(fields)]
    for z in range(depth):
        beside = spread(packed, z)
        here = (row >= 2 * z) & (row < 2 * z + 2)
        for f in range(fields):
            both = jnp.concatenate([raw_ref[f, z], beside[f * rows:(f + 1) * rows]], axis=1)
            upper = pltpu.roll(both[:8], 2 * z, 0)
            lower = pltpu.roll(both[rows - 8:], (2 * z + 2) % 8, 0)
            lines[f] = jnp.where(here, jnp.where(even_y, upper, lower), lines[f])
    for f in range(fields):
        line_ref[f] = lines[f]


def wave_kernel(where_ref, own_ref, other_ref, near_ref, far_ref, pair_ref):
    fields = near_ref.shape[0]
    depth = own_ref.shape[0] // fields - 1
    half = own_ref.shape[1]
    rows = 2 * half
    width = 2 * LANES
    high_rows = rows + 8
    lane = lax.broadcasted_iota(jnp.int32, (rows, LANES), 1)
    edge_row = lax.broadcasted_iota(jnp.int32, (8, width), 0)
    even_y = where_ref[2] == 0

    def ordered(mine, other):
        return [jnp.where(even_y, mine, other), jnp.where(even_y, other, mine)]

    packed_all = []
    for f in range(fields):
        packed_all += ordered(own_ref[fields * depth + f], other_ref[fields * depth + f])
    packed_all = jnp.concatenate(packed_all, axis=0)
    besides = [spread(packed_all, z) for z in range(depth)]
    top = [jnp.where(even_y, near_ref[f], far_ref[f]) for f in range(fields)]
    bottom = [jnp.where(even_y, far_ref[f], near_ref[f]) for f in range(fields)]

    def whole(f, z):
        edge = jnp.where(edge_row >= 6, pltpu.roll(top[f], (6 - 2 * z) % 8, 0), 0.0)
        edge = jnp.where(edge_row < 2, pltpu.roll(bottom[f], (8 - 2 * z) % 8, 0), edge)
        plane = f * depth + z
        body = jnp.concatenate(ordered(own_ref[plane], other_ref[plane]), axis=0)
        beside = besides[z][f * rows:(f + 1) * rows]
        both = jnp.concatenate([body, beside], axis=1)
        return jnp.concatenate([both, edge], axis=0)

    speed = [whole(4, z) for z in range(depth)]

    def advance(prev, now):
        out = []
        for z in range(depth):
            c = now[z]
            near = pltpu.roll(c, 1, 0) + pltpu.roll(c, high_rows - 1, 0)
            near = near + pltpu.roll(c, 1, 1) + pltpu.roll(c, width - 1, 1)
            if z > 0:
                near = near + now[z - 1]
            if z < depth - 1:
                near = near + now[z + 1]
            out.append(2.0 * c - prev[z] + speed[z] * (near - 6.0 * c))
        return out

    packed = [jnp.zeros((rows, LANES), jnp.float32) for _ in range(2)]
    for pair in range(2):
        prev = [whole(2 * pair, z) for z in range(depth)]
        now = [whole(2 * pair + 1, z) for z in range(depth)]
        for t in range(STEPS):
            prev, now = now, advance(prev, now)
            for z in range(depth):
                plane = (pair * STEPS + t) * depth + z
                q = plane % 8
                for k in range(2):
                    pair_ref[k, plane] = now[z][k * half:(k + 1) * half, :LANES]
                beside = roll_lanes(now[z][:rows, LANES:], 8 + 16 * q)
                here = (lane >= 16 * q) & (lane < 16 * q + 16)
                packed[plane // 8] = jnp.where(here, beside, packed[plane // 8])
    for j in range(2):
        for k in range(2):
            pair_ref[k, 4 * depth + j] = packed[j][k * half:(k + 1) * half]


def needed(call):
    return sorted({r for r, _, _ in call} | {(r + k) % 8 for r, a, m in call for k in (-1, 1)
                   if (k < 0 and a == 0) or (k > 0 and a + m == 32)})


def image_kernel(call, first, last, *refs):
    refs = list(refs)
    where_ref, shifts_ref, observed_ref = refs[:3]
    del refs[:4 if first else 3]
    tiles = {}
    for r in needed(call):
        tiles[r], refs = refs[:2], refs[2:]
    if not first:
        refs = refs[1:]
    segments = list(call)
    earlier = []
    if last:
        for other in CALLS:
            if other != call:
                for segment in other:
                    earlier.append((segment, refs[0], refs[1]))
                    refs = refs[2:]
    n_seg = len(segments)
    image_hbm, refs = refs[0], refs[1:]
    if last:
        core_out, send_in, send_out = refs[:3]
        refs = refs[3:]
    sums = []
    for _ in segments:
        sums.append(refs[:2])
        refs = refs[2:]
    mains, sides, images = refs[:n_seg], refs[n_seg:2 * n_seg], refs[2 * n_seg:3 * n_seg]
    sems = refs[3 * n_seg]
    count, depth, all_rows = observed_ref.shape[:3]
    planes = 4 * depth
    rows = all_rows // 8
    half = rows // 2

    def z_of(r):
        return lax.rem(where_ref[0] + r, 8)

    def put(n, part):
        r, a, m = segments[n]
        at = pl.multiple_of(z_of(r) * rows + a, 8)
        which = pl.ds(part * GROUP, GROUP)
        return pltpu.make_async_copy(
            images[n].at[which, :, pl.ds(0, m), :],
            image_hbm.at[which, :, pl.ds(at, m), :],
            sems.at[n, part],
        )

    packs, homes = [], []
    for n, (r, a, m) in enumerate(segments):
        for ref in sums[n]:
            ref[...] = jnp.zeros_like(ref)
        for b in range(a - HMAX, a + m + HMAX, 8):
            step = -1 if b < 0 else (1 if b >= rows else 0)
            b_in = b - step * rows
            ref = tiles[(r + step) % 8][b_in // half]
            part = slice(b_in % half, b_in % half + 8)
            inside = {-1: z_of(r) > 0, 0: None, 1: z_of(r) < 7}[step]
            to = slice(b - a + HMAX, b - a + HMAX + 8)

            def load(p):
                value = ref[p, part, :]
                return value if inside is None else jnp.where(inside, value, 0.0)

            for p in range(planes):
                mains[n][p, to, :] = load(p)
            for k in range(2):
                packs.append(load(planes + k))
                homes.append((n, 8 * k, to))
    packs = jnp.concatenate(packs, axis=0)
    for q in range(8):
        turned = roll_lanes(packs, -(8 + 16 * q))
        for i, (n, p, to) in enumerate(homes):
            sides[n][p + q, to, :] = turned[8 * i:8 * i + 8]

    lane = lax.broadcasted_iota(jnp.int32, (rows, LANES), 1)

    def rotated(pieces, amount):
        turned = pltpu.roll(jnp.concatenate(pieces, axis=0), amount, 1)
        out, at = [], 0
        for x in pieces:
            out.append(turned[at:at + x.shape[0]])
            at += x.shape[0]
        return out

    def per_offset(o):
        hx = shifts_ref[o, 0]
        hy = shifts_ref[o, 1]
        wrap_s = (lane < -hx) | (lane >= LANES - hx)
        wrap_r = (lane < hx) | (lane >= LANES + hx)
        to_s = lax.rem(hx + LANES, LANES)
        to_r = lax.rem(LANES - hx, LANES)
        s_at = HMAX - hy
        r_at = HMAX + hy

        def piece(n, plane, start, wrap):
            m = segments[n][2]
            a = mains[n][plane, pl.ds(start, m), :]
            return jnp.where(wrap[:m], sides[n][plane, pl.ds(start, m), :], a)

        parts = [(n, z) for n in range(n_seg) for z in range(depth)]
        sources, receivers, observed = [], [], []
        for n, z in parts:
            r, a, m = segments[n]
            for t in range(STEPS):
                sources.append(piece(n, t * depth + z, s_at, wrap_s))
                receivers.append(piece(n, (STEPS + t) * depth + z, r_at, wrap_r))
            lead = a % half
            y_at = pl.multiple_of(z_of(r) * rows + a - lead, half)
            seen = observed_ref[o, z, pl.ds(y_at, whole_tiles(lead + m)), :]
            observed.append(seen.astype(jnp.float32)[lead:lead + m])
        sources = rotated(sources, lax.rem(2 * hx + LANES, LANES))
        observed = rotated(observed, to_s)
        fulls, terms = [], []
        for i in range(len(parts)):
            s1, s2 = sources[2 * i:2 * i + 2]
            r1, r2 = receivers[2 * i:2 * i + 2]
            full = s1 * r1 + s2 * r2
            fulls.append(full)
            terms.append((full - observed[i]) * s2)
        for (n, z), full in zip(parts, rotated(fulls, to_r)):
            images[n][o, z, :segments[n][2]] = full.astype(jnp.bfloat16)
        kept = []
        for (n, z), t in zip(parts, terms):
            m = segments[n][2]
            at = (z, pl.ds(r_at, m))
            inner = sums[n][0][at] + jnp.where(wrap_r[:m], 0.0, t)
            outer = sums[n][1][at] + jnp.where(wrap_r[:m], t, 0.0)
            kept.append((n, at, inner, outer))
        for n, at, inner, outer in kept:
            sums[n][0][at] = inner
            sums[n][1][at] = outer

    def per_group(part, carry):
        for k in range(GROUP):
            per_offset(part * GROUP + k)
        for n in range(n_seg):
            put(n, part).start()
        return carry

    lax.fori_loop(0, count // GROUP, per_group, 0)

    if last:
        all_core, all_side = refs[3 * n_seg + 1:]
        all_core[...] = jnp.zeros_like(all_core)
        all_side[...] = jnp.zeros_like(all_side)
        mine = [(segment, c, e) for segment, (c, e) in zip(segments, sums)]
        for (r, a, m), c, e in earlier + mine:
            at = pl.multiple_of(z_of(r) * rows + a, 8)
            all_core[:, pl.ds(at, m + 2 * HMAX), :] += c[...]
            all_side[:, pl.ds(at, m + 2 * HMAX), :] += e[...]
        n_tiles = all_rows // half
        for tile in range(n_tiles):
            at = HMAX + tile * half
            for z in range(depth):
                core_out[tile, z * half:(z + 1) * half, :] = all_core[z, at:at + half, :]
        lane8 = lax.broadcasted_iota(jnp.int32, (8 * n_tiles, LANES), 1)
        strip = jnp.zeros((8 * n_tiles, LANES), jnp.float32)
        for q in range(8):
            z, k = q % 4, q // 4
            starts = [HMAX + tile * half + 8 * k for tile in range(n_tiles)]
            part = jnp.concatenate([all_side[z, at:at + 8, :] for at in starts], axis=0)
            here = (lane8 >= 16 * q) & (lane8 < 16 * q + 16)
            strip = jnp.where(here, roll_lanes(part, 8 + 16 * q), strip)
        cut = 4 * n_tiles
        low = lax.rem(lane8[:cut], 16) < HMAX
        lefts = jnp.where(low, strip[:cut], roll_lanes(strip[cut:], HMAX))
        rights = jnp.where(low, roll_lanes(strip[:cut], -HMAX), strip[cut:])
        even_x = where_ref[1] == 0
        send_in[...] = jnp.where(even_x, rights, lefts)
        send_out[...] = jnp.where(even_x, lefts, rights)
    for n in range(n_seg):
        for part in range(count // GROUP):
            put(n, part).wait()


def merge_kernel(where_ref, core_ref, inner_ref, outer_ref, out_ref):
    n_tiles = core_ref.shape[0]
    cut = inner_ref.shape[0]
    even_x = where_ref[1] == 0
    from_right = jnp.where(even_x, inner_ref[...], outer_ref[...])
    from_left = jnp.where(even_x, outer_ref[...], inner_ref[...])
    lane = lax.broadcasted_iota(jnp.int32, (cut, LANES), 1)
    for group in range(2):
        for q in range(8):
            slot = 16 * q + HMAX * group
            extra = jnp.where(lane < HMAX, roll_lanes(from_left, -slot), 0.0)
            extra = jnp.where(lane >= LANES - HMAX, roll_lanes(from_right, 120 - slot), extra)
            at = (q % 4) * 16 + (q // 4) * 8
            for i in range(n_tiles // 2):
                tile = group * (n_tiles // 2) + i
                out_ref[tile, at:at + 8, :] = core_ref[tile, at:at + 8, :] + extra[8 * i:8 * i + 8]


def total_kernel(parts_ref, out_ref):
    total = parts_ref[0]
    for i in range(1, parts_ref.shape[0]):
        total = total + parts_ref[i]
    rows = out_ref.shape[1]
    for z in range(out_ref.shape[0]):
        out_ref[z] = total[z * rows:(z + 1) * rows] * (1.0 / OFF_SIDE)


def on_device(src_prev, src_now, rcv_prev, rcv_now, velocity, shift_table, ref_image):
    depth, rows, cols = src_now.shape
    n_off = lax.axis_size("offset")
    n_space = lax.axis_size("space")
    all_rows = ref_image.shape[2]
    shape = jax.ShapeDtypeStruct
    f32 = jnp.float32
    whole = pl.BlockSpec(memory_space=pltpu.VMEM)
    scalars = pl.BlockSpec(memory_space=pltpu.SMEM)
    anywhere = pl.BlockSpec(memory_space=pl.ANY)
    me = lax.axis_index("offset")
    where = jnp.stack([me // 2, lax.axis_index("space") % 2, me % 2]).astype(jnp.int32)

    raw, edge = pl.pallas_call(
        edges_kernel,
        out_shape=[shape((5, depth, rows, cols), f32), shape((5, rows, cols), f32)],
        name="edges",
    )(src_prev, src_now, rcv_prev, rcv_now, velocity)
    inner_x, outer_x = swaps(n_space)
    inner_y, outer_y = swaps(n_off)
    same_y = [(i, i + 2 if i % 2 else i - 2) for i in range(n_off)]
    same_y = [(i, j) for i, j in same_y if 0 <= j < n_off]
    got_in = lax.ppermute(edge, "space", inner_x)
    got_out = lax.ppermute(edge, "space", outer_x)
    raw = pl.pallas_call(
        hold_kernel,
        in_specs=[whole],
        out_specs=whole,
        out_shape=shape(raw.shape, f32),
        compiler_params=SMALL,
        cost_estimate=pl.CostEstimate(flops=0, bytes_accessed=4_000_000, transcendentals=0),
        name="hold",
    )(raw)
    own, line = pl.pallas_call(
        widen_kernel,
        in_specs=[scalars] * 2 + [whole] * 3,
        out_shape=[shape((5 * depth + 5, rows, cols), f32), shape((5, 8, 2 * LANES), f32)],
        name="widen", compiler_params=SMALL,
    )(where, shift_table, raw, got_in, got_out)
    other = lax.ppermute(own, "offset", inner_y)
    near = lax.ppermute(line, "offset", outer_y)
    far = lax.ppermute(line, "offset", same_y)
    planes = 4 * depth + 2
    pair = pl.pallas_call(
        wave_kernel,
        in_specs=[scalars] + [whole] * 4,
        out_shape=shape((2, planes, rows, LANES), f32),
        name="wave", compiler_params=SMALL,
    )(where, own, other, near, far)

    def turn(d):
        return [(i, (i - 2 * d) % n_off) for i in range(n_off)]

    tiles = [(pair[0], pair[1])] + [None] * 7
    touched = pl.pallas_call(
        touch_kernel,
        in_specs=[whole],
        out_specs=whole,
        out_shape=shape((8, LANES), f32),
        compiler_params=SMALL,
        cost_estimate=pl.CostEstimate(flops=0, bytes_accessed=8_000_000, transcendentals=0),
        name="touch",
    )(ref_image)
    local = shift_table.shape[0]
    image = None
    done = []
    up = down = pair
    for at, call in enumerate(CALLS):
        first, last = call == CALLS[0], call == CALLS[-1]
        if first:
            up = lax.ppermute(pair, "offset", turn(1))
            down = lax.ppermute(pair, "offset", turn(-1))
            up, down, touched = lax.optimization_barrier((up, down, touched))
            tiles[1], tiles[7] = (up[0], up[1]), (down[0], down[1])
        if at < 2:
            next_up = lax.ppermute(up, "offset", turn(1))
            next_down = lax.ppermute(down, "offset", turn(-1))
        elif at == 2:
            next_up = lax.ppermute(up[0], "offset", turn(1))
            next_down = lax.ppermute(down[1], "offset", turn(-1))
        args = [where, shift_table, ref_image]
        specs = [scalars, scalars, whole]
        if first:
            args.append(touched)
            specs.append(whole)
        for r in needed(call):
            args += tiles[r]
            specs += [whole, whole]
        aliases = {}
        if not first:
            aliases = {len(args): 0}
            args.append(image)
            specs.append(anywhere)
        sums = [(depth, m + 2 * HMAX, LANES) for _, _, m in call for _ in range(2)]
        fields = [pltpu.VMEM((4 * depth, m + 2 * HMAX, LANES), f32) for _, _, m in call]
        scratch = fields + fields
        scratch += [pltpu.VMEM((local, depth, whole_tiles(m), LANES), jnp.bfloat16) for _, _, m in call]
        scratch += [pltpu.SemaphoreType.DMA((len(call), local // GROUP))]
        if last:
            args += done
            specs += [whole] * len(done)
            scratch = [pltpu.VMEM(dims, f32) for dims in sums] + scratch
            scratch += [pltpu.VMEM((depth, all_rows + 2 * HMAX, LANES), f32)] * 2
            half_strip = shape((n_off * 4, LANES), f32)
            outs = [shape((n_off, depth * rows, LANES), f32), half_strip, half_strip]
        else:
            outs = [shape(dims, f32) for dims in sums]
        image, *rest = pl.pallas_call(
            functools.partial(image_kernel, call, first, last),
            in_specs=specs,
            out_specs=[anywhere] + [whole] * len(outs),
            out_shape=[shape(ref_image.shape, jnp.bfloat16)] + outs,
            scratch_shapes=scratch,
            input_output_aliases=aliases,
            compiler_params=pltpu.CompilerParams(vmem_limit_bytes=16 * 2**20),
            cost_estimate=pl.CostEstimate(
                flops=20_000_000, bytes_accessed=8_000_000, transcendentals=0
            ),
            name="image",
        )(*args)
        done += rest
        if not last:
            up, down, image = lax.optimization_barrier((next_up, next_down, image))
            if at < 2:
                tiles[at + 2], tiles[6 - at] = (up[0], up[1]), (down[0], down[1])
            else:
                tiles[4] = (up, down)

    core, send_in, send_out = rest
    got_in = lax.ppermute(send_in, "space", inner_x)
    got_out = lax.ppermute(send_out, "space", outer_x)
    parts = pl.pallas_call(
        merge_kernel,
        in_specs=[scalars] + [whole] * 3,
        out_shape=shape(core.shape, f32),
        name="merge", compiler_params=SMALL,
    )(where, core, got_in, got_out)
    parts = lax.all_to_all(parts, "offset", 0, 0)
    adjoint = pl.pallas_call(
        total_kernel, out_shape=shape((depth, rows, cols), f32), name="total", compiler_params=SMALL
    )(parts)
    return image, adjoint


def solution(mesh):
    field = P(None, "offset", "space")
    in_specs = (field,) * 5 + (P("offset", None), P("offset", None, None, "space"))
    out_specs = (P("offset", None, None, "space"), field)
    return jax.shard_map(
        on_device, mesh=mesh, in_specs=in_specs, out_specs=out_specs, check_vma=False
    )
```

```python
import functools

import jax
import jax.numpy as jnp
from jax import lax
from jax.experimental import pallas as pl
from jax.experimental.pallas import tpu as pltpu
from jax.sharding import PartitionSpec as P

OFF_SIDE = 16
HMAX = 8
STEPS = 2
REACH = HMAX + STEPS
LANES = 128
GROUP = 8
SMALL = pltpu.CompilerParams(vmem_limit_bytes=6 * 2**20)

CALLS = (
    ((7, 8, 24), (0, 0, 32), (1, 0, 24)),
    ((1, 24, 8), (2, 0, 24), (6, 8, 24), (7, 0, 8)),
    ((2, 24, 8), (3, 0, 24), (5, 8, 24), (6, 0, 8)),
    ((3, 24, 8), (4, 0, 32), (5, 0, 8)),
)


def swaps(count):
    inner = [(i, i ^ 1) for i in range(count)]
    outer = [(i, i + 1 if i % 2 else i - 1) for i in range(1, count - 1)]
    return inner, outer


def whole_tiles(rows):
    return -(-rows // 16) * 16


def roll_lanes(x, shift):
    return pltpu.roll(x, shift % LANES, x.ndim - 1)


def edges_kernel(*refs):
    fields, raw_ref, edge_ref = refs[:-2], refs[-2], refs[-1]
    depth, rows, cols = fields[0].shape
    total = len(fields) * rows
    lane = lax.broadcasted_iota(jnp.int32, (total, LANES), 1)
    packed = jnp.zeros((total, LANES), jnp.float32)
    for z in range(depth):
        plane = jnp.concatenate([ref[z] for ref in fields], axis=0)
        for f in range(len(fields)):
            raw_ref[f, z] = plane[f * rows:(f + 1) * rows]
        first = roll_lanes(plane, 32 * z)
        last = roll_lanes(plane, 32 * z + 32)
        packed = jnp.where((lane >= 32 * z) & (lane < 32 * z + 16), first, packed)
        packed = jnp.where((lane >= 32 * z + 16) & (lane < 32 * z + 32), last, packed)
    for f in range(len(fields)):
        edge_ref[f] = packed[f * rows:(f + 1) * rows]


def hold_kernel(ref, out_ref):
    out_ref[...] = ref[...]


def touch_kernel(shifts_ref, ref, out_ref):
    out_ref[...] = ref[0, 0, :8, :].astype(jnp.float32)


def spread(packed, z):
    lane = lax.broadcasted_iota(jnp.int32, packed.shape, 1)
    beside = jnp.where(lane >= LANES - REACH, roll_lanes(packed, 96 - 32 * z), 0.0)
    return jnp.where(lane < REACH, roll_lanes(packed, -32 * z), beside)


def widen_kernel(where_ref, raw_ref, inner_ref, outer_ref, own_ref, line_ref):
    fields, depth, rows, cols = raw_ref.shape
    lane = lax.broadcasted_iota(jnp.int32, (fields * rows, LANES), 1)
    row = lax.broadcasted_iota(jnp.int32, (8, 2 * LANES), 0)
    even_x = where_ref[1] == 0
    even_y = where_ref[2] == 0
    inner = jnp.concatenate([inner_ref[f] for f in range(fields)], axis=0)
    outer = jnp.concatenate([outer_ref[f] for f in range(fields)], axis=0)
    left = jnp.where(even_x, outer, inner)
    right = jnp.where(even_x, inner, outer)
    packed = jnp.where(lax.rem(lane, 32) < 16, right, left)
    for f in range(fields):
        own_ref[fields * depth + f] = packed[f * rows:(f + 1) * rows]
        for z in range(depth):
            own_ref[f * depth + z] = raw_ref[f, z]
    lines = [jnp.zeros((8, 2 * LANES), jnp.float32) for _ in range(fields)]
    first = jnp.concatenate([packed[f * rows:f * rows + 8] for f in range(fields)], axis=0)
    last = jnp.concatenate([packed[(f + 1) * rows - 8:(f + 1) * rows] for f in range(fields)], axis=0)
    packed = jnp.where(even_y, first, last)
    for z in range(depth):
        beside = spread(packed, z)
        here = (row >= 2 * z) & (row < 2 * z + 2)
        to = jnp.where(even_y, 2 * z, (2 * z + 2) % 8)
        both = []
        for f in range(fields):
            edge = jnp.where(even_y, raw_ref[f, z, :8], raw_ref[f, z, rows - 8:])
            both.append(jnp.concatenate([edge, beside[8 * f:8 * f + 8]], axis=1))
        for f in range(fields):
            lines[f] = jnp.where(here, pltpu.roll(both[f], to, 0), lines[f])
    for f in range(fields):
        line_ref[f] = lines[f]


def wave_kernel(where_ref, own_ref, other_ref, near_ref, far_ref, pair_ref):
    fields = near_ref.shape[0]
    depth = own_ref.shape[0] // fields - 1
    half = own_ref.shape[1]
    rows = 2 * half
    width = 2 * LANES
    high_rows = rows + 8
    lane = lax.broadcasted_iota(jnp.int32, (rows, LANES), 1)
    edge_row = lax.broadcasted_iota(jnp.int32, (8, width), 0)
    even_y = where_ref[2] == 0

    def ordered(mine, other):
        return [jnp.where(even_y, mine, other), jnp.where(even_y, other, mine)]

    packed_all = []
    for f in range(fields):
        packed_all += ordered(own_ref[fields * depth + f], other_ref[fields * depth + f])
    packed_all = jnp.concatenate(packed_all, axis=0)
    besides = [spread(packed_all, z) for z in range(depth)]
    top = [jnp.where(even_y, near_ref[f], far_ref[f]) for f in range(fields)]
    bottom = [jnp.where(even_y, far_ref[f], near_ref[f]) for f in range(fields)]

    def whole(f, z):
        edge = jnp.where(edge_row >= 6, pltpu.roll(top[f], (6 - 2 * z) % 8, 0), 0.0)
        edge = jnp.where(edge_row < 2, pltpu.roll(bottom[f], (8 - 2 * z) % 8, 0), edge)
        plane = f * depth + z
        body = jnp.concatenate(ordered(own_ref[plane], other_ref[plane]), axis=0)
        beside = besides[z][f * rows:(f + 1) * rows]
        both = jnp.concatenate([body, beside], axis=1)
        return jnp.concatenate([both, edge], axis=0)

    speed = [whole(4, z) for z in range(depth)]

    def advance(prev, now):
        out = []
        for z in range(depth):
            c = now[z]
            near = pltpu.roll(c, 1, 0) + pltpu.roll(c, high_rows - 1, 0)
            near = near + pltpu.roll(c, 1, 1) + pltpu.roll(c, width - 1, 1)
            if z > 0:
                near = near + now[z - 1]
            if z < depth - 1:
                near = near + now[z + 1]
            out.append(2.0 * c - prev[z] + speed[z] * (near - 6.0 * c))
        return out

    packed = [jnp.zeros((rows, LANES), jnp.float32) for _ in range(2)]
    for pair in range(2):
        prev = [whole(2 * pair, z) for z in range(depth)]
        now = [whole(2 * pair + 1, z) for z in range(depth)]
        for t in range(STEPS):
            prev, now = now, advance(prev, now)
            for z in range(depth):
                plane = (pair * STEPS + t) * depth + z
                q = plane % 8
                for k in range(2):
                    pair_ref[k, plane] = now[z][k * half:(k + 1) * half, :LANES]
                beside = roll_lanes(now[z][:rows, LANES:], 8 + 16 * q)
                here = (lane >= 16 * q) & (lane < 16 * q + 16)
                packed[plane // 8] = jnp.where(here, beside, packed[plane // 8])
    for j in range(2):
        for k in range(2):
            pair_ref[k, 4 * depth + j] = packed[j][k * half:(k + 1) * half]


def needed(call):
    return sorted({r for r, _, _ in call} | {(r + k) % 8 for r, a, m in call for k in (-1, 1)
                   if (k < 0 and a == 0) or (k > 0 and a + m == 32)})


def image_kernel(call, first, last, *refs):
    refs = list(refs)
    where_ref, shifts_ref, observed_ref = refs[:3]
    del refs[:4 if first else 3]
    tiles = {}
    for r in needed(call):
        tiles[r], refs = refs[:2], refs[2:]
    if not first:
        refs = refs[1:]
    segments = list(call)
    earlier = []
    if last:
        for other in CALLS:
            if other != call:
                for segment in other:
                    earlier.append((segment, refs[0], refs[1]))
                    refs = refs[2:]
    n_seg = len(segments)
    image_hbm, refs = refs[0], refs[1:]
    if last:
        core_out, send_in, send_out = refs[:3]
        refs = refs[3:]
    sums = []
    for _ in segments:
        sums.append(refs[:2])
        refs = refs[2:]
    mains, sides, images = refs[:n_seg], refs[n_seg:2 * n_seg], refs[2 * n_seg:3 * n_seg]
    sems = refs[3 * n_seg]
    count, depth, all_rows = observed_ref.shape[:3]
    planes = 4 * depth
    rows = all_rows // 8
    half = rows // 2

    def z_of(r):
        return lax.rem(where_ref[0] + r, 8)

    def put(n, part):
        r, a, m = segments[n]
        at = pl.multiple_of(z_of(r) * rows + a, 8)
        which = pl.ds(part * GROUP, GROUP)
        return pltpu.make_async_copy(
            images[n].at[which, :, pl.ds(0, m), :],
            image_hbm.at[which, :, pl.ds(at, m), :],
            sems.at[n, part],
        )

    packs, homes = [], []
    for n, (r, a, m) in enumerate(segments):
        for ref in sums[n]:
            ref[...] = jnp.zeros_like(ref)
        for b in range(a - HMAX, a + m + HMAX, 8):
            step = -1 if b < 0 else (1 if b >= rows else 0)
            b_in = b - step * rows
            ref = tiles[(r + step) % 8][b_in // half]
            part = slice(b_in % half, b_in % half + 8)
            inside = {-1: z_of(r) > 0, 0: None, 1: z_of(r) < 7}[step]
            to = slice(b - a + HMAX, b - a + HMAX + 8)

            def load(p):
                value = ref[p, part, :]
                return value if inside is None else jnp.where(inside, value, 0.0)

            for p in range(planes):
                mains[n][p, to, :] = load(p)
            for k in range(2):
                packs.append(load(planes + k))
                homes.append((n, 8 * k, to))
    packs = jnp.concatenate(packs, axis=0)
    for q in range(8):
        turned = roll_lanes(packs, -(8 + 16 * q))
        for i, (n, p, to) in enumerate(homes):
            sides[n][p + q, to, :] = turned[8 * i:8 * i + 8]

    lane = lax.broadcasted_iota(jnp.int32, (rows, LANES), 1)

    def rotated(pieces, amount):
        turned = pltpu.roll(jnp.concatenate(pieces, axis=0), amount, 1)
        out, at = [], 0
        for x in pieces:
            out.append(turned[at:at + x.shape[0]])
            at += x.shape[0]
        return out

    def per_offset(o):
        hx = shifts_ref[o, 0]
        hy = shifts_ref[o, 1]
        wrap_s = (lane < -hx) | (lane >= LANES - hx)
        wrap_r = (lane < hx) | (lane >= LANES + hx)
        to_s = lax.rem(hx + LANES, LANES)
        to_r = lax.rem(LANES - hx, LANES)
        s_at = HMAX - hy
        r_at = HMAX + hy

        def piece(n, plane, start, wrap):
            m = segments[n][2]
            a = mains[n][plane, pl.ds(start, m), :]
            return jnp.where(wrap[:m], sides[n][plane, pl.ds(start, m), :], a)

        parts = [(n, z) for n in range(n_seg) for z in range(depth)]
        sources, receivers, observed = [], [], []
        for n, z in parts:
            r, a, m = segments[n]
            for t in range(STEPS):
                sources.append(piece(n, t * depth + z, s_at, wrap_s))
                receivers.append(piece(n, (STEPS + t) * depth + z, r_at, wrap_r))
            lead = a % half
            y_at = pl.multiple_of(z_of(r) * rows + a - lead, half)
            seen = observed_ref[o, z, pl.ds(y_at, whole_tiles(lead + m)), :]
            observed.append(seen.astype(jnp.float32)[lead:lead + m])
        sources = rotated(sources, lax.rem(2 * hx + LANES, LANES))
        observed = rotated(observed, to_s)
        fulls, terms = [], []
        for i in range(len(parts)):
            s1, s2 = sources[2 * i:2 * i + 2]
            r1, r2 = receivers[2 * i:2 * i + 2]
            full = s1 * r1 + s2 * r2
            fulls.append(full)
            terms.append((full - observed[i]) * s2)
        for (n, z), full in zip(parts, rotated(fulls, to_r)):
            images[n][o, z, :segments[n][2]] = full.astype(jnp.bfloat16)
        kept = []
        for (n, z), t in zip(parts, terms):
            m = segments[n][2]
            at = (z, pl.ds(r_at, m))
            inner = sums[n][0][at] + jnp.where(wrap_r[:m], 0.0, t)
            outer = sums[n][1][at] + jnp.where(wrap_r[:m], t, 0.0)
            kept.append((n, at, inner, outer))
        for n, at, inner, outer in kept:
            sums[n][0][at] = inner
            sums[n][1][at] = outer

    def per_group(part, carry):
        for k in range(GROUP):
            per_offset(part * GROUP + k)
        for n in range(n_seg):
            put(n, part).start()
        return carry

    lax.fori_loop(0, count // GROUP, per_group, 0)

    if last:
        all_core, all_side = refs[3 * n_seg + 1:]
        all_core[...] = jnp.zeros_like(all_core)
        all_side[...] = jnp.zeros_like(all_side)
        mine = [(segment, c, e) for segment, (c, e) in zip(segments, sums)]
        for (r, a, m), c, e in earlier + mine:
            at = pl.multiple_of(z_of(r) * rows + a, 8)
            all_core[:, pl.ds(at, m + 2 * HMAX), :] += c[...]
            all_side[:, pl.ds(at, m + 2 * HMAX), :] += e[...]
        n_tiles = all_rows // half
        for tile in range(n_tiles):
            at = HMAX + tile * half
            for z in range(depth):
                core_out[tile, z * half:(z + 1) * half, :] = all_core[z, at:at + half, :]
        lane8 = lax.broadcasted_iota(jnp.int32, (8 * n_tiles, LANES), 1)
        strip = jnp.zeros((8 * n_tiles, LANES), jnp.float32)
        for q in range(8):
            z, k = q % 4, q // 4
            starts = [HMAX + tile * half + 8 * k for tile in range(n_tiles)]
            part = jnp.concatenate([all_side[z, at:at + 8, :] for at in starts], axis=0)
            here = (lane8 >= 16 * q) & (lane8 < 16 * q + 16)
            strip = jnp.where(here, roll_lanes(part, 8 + 16 * q), strip)
        cut = 4 * n_tiles
        low = lax.rem(lane8[:cut], 16) < HMAX
        lefts = jnp.where(low, strip[:cut], roll_lanes(strip[cut:], HMAX))
        rights = jnp.where(low, roll_lanes(strip[:cut], -HMAX), strip[cut:])
        even_x = where_ref[1] == 0
        send_in[...] = jnp.where(even_x, rights, lefts)
        send_out[...] = jnp.where(even_x, lefts, rights)
    for n in range(n_seg):
        for part in range(count // GROUP):
            put(n, part).wait()


def merge_kernel(where_ref, core_ref, inner_ref, outer_ref, out_ref):
    n_tiles = core_ref.shape[0]
    cut = inner_ref.shape[0]
    even_x = where_ref[1] == 0
    from_right = jnp.where(even_x, inner_ref[...], outer_ref[...])
    from_left = jnp.where(even_x, outer_ref[...], inner_ref[...])
    both = jnp.concatenate([from_left, roll_lanes(from_right, LANES - HMAX)], axis=0)
    lane = lax.broadcasted_iota(jnp.int32, (cut, LANES), 1)
    for group in range(2):
        for q in range(8):
            turned = roll_lanes(both, -(16 * q + HMAX * group))
            extra = jnp.where(lane < HMAX, turned[:cut], 0.0)
            extra = jnp.where(lane >= LANES - HMAX, turned[cut:], extra)
            at = (q % 4) * 16 + (q // 4) * 8
            for i in range(n_tiles // 2):
                tile = group * (n_tiles // 2) + i
                out_ref[tile, at:at + 8, :] = core_ref[tile, at:at + 8, :] + extra[8 * i:8 * i + 8]


def total_kernel(parts_ref, out_ref):
    total = parts_ref[0]
    for i in range(1, parts_ref.shape[0]):
        total = total + parts_ref[i]
    rows = out_ref.shape[1]
    for z in range(out_ref.shape[0]):
        out_ref[z] = total[z * rows:(z + 1) * rows] * (1.0 / OFF_SIDE)


def on_device(src_prev, src_now, rcv_prev, rcv_now, velocity, shift_table, ref_image):
    depth, rows, cols = src_now.shape
    n_off = lax.axis_size("offset")
    n_space = lax.axis_size("space")
    all_rows = ref_image.shape[2]
    shape = jax.ShapeDtypeStruct
    f32 = jnp.float32
    whole = pl.BlockSpec(memory_space=pltpu.VMEM)
    scalars = pl.BlockSpec(memory_space=pltpu.SMEM)
    anywhere = pl.BlockSpec(memory_space=pl.ANY)
    me = lax.axis_index("offset")
    where = jnp.stack([me // 2, lax.axis_index("space") % 2, me % 2]).astype(jnp.int32)

    raw, edge = pl.pallas_call(
        edges_kernel,
        out_shape=[shape((5, depth, rows, cols), f32), shape((5, rows, cols), f32)],
        name="edges",
    )(src_prev, src_now, rcv_prev, rcv_now, velocity)
    inner_x, outer_x = swaps(n_space)
    inner_y, outer_y = swaps(n_off)
    same_y = [(i, i + 2 if i % 2 else i - 2) for i in range(n_off)]
    same_y = [(i, j) for i, j in same_y if 0 <= j < n_off]
    got_in = lax.ppermute(edge, "space", inner_x)
    got_out = lax.ppermute(edge, "space", outer_x)
    raw = pl.pallas_call(
        hold_kernel,
        in_specs=[whole],
        out_specs=whole,
        out_shape=shape(raw.shape, f32),
        compiler_params=SMALL,
        cost_estimate=pl.CostEstimate(flops=0, bytes_accessed=4_000_000, transcendentals=0),
        name="hold",
    )(raw)
    own, line = pl.pallas_call(
        widen_kernel,
        in_specs=[scalars] + [whole] * 3,
        out_shape=[shape((5 * depth + 5, rows, cols), f32), shape((5, 8, 2 * LANES), f32)],
        name="widen", compiler_params=SMALL,
    )(where, raw, got_in, got_out)
    other = lax.ppermute(own, "offset", inner_y)
    near = lax.ppermute(line, "offset", outer_y)
    far = lax.ppermute(line, "offset", same_y)
    planes = 4 * depth + 2
    pair = pl.pallas_call(
        wave_kernel,
        in_specs=[scalars] + [whole] * 4,
        out_shape=shape((2, planes, rows, LANES), f32),
        name="wave", compiler_params=SMALL,
    )(where, own, other, near, far)

    def turn(d):
        return [(i, (i - 2 * d) % n_off) for i in range(n_off)]

    tiles = [(pair[0], pair[1])] + [None] * 7
    touched = pl.pallas_call(
        touch_kernel,
        in_specs=[scalars, whole],
        out_specs=whole,
        out_shape=shape((8, LANES), f32),
        compiler_params=SMALL,
        cost_estimate=pl.CostEstimate(flops=0, bytes_accessed=8_000_000, transcendentals=0),
        name="touch",
    )(shift_table, ref_image)
    local = shift_table.shape[0]
    image = None
    done = []
    up = down = pair
    for at, call in enumerate(CALLS):
        first, last = call == CALLS[0], call == CALLS[-1]
        if first:
            up = lax.ppermute(pair, "offset", turn(1))
            down = lax.ppermute(pair, "offset", turn(-1))
            up, down, touched = lax.optimization_barrier((up, down, touched))
            tiles[1], tiles[7] = (up[0], up[1]), (down[0], down[1])
        if at < 2:
            next_up = lax.ppermute(up, "offset", turn(1))
            next_down = lax.ppermute(down, "offset", turn(-1))
        elif at == 2:
            next_up = lax.ppermute(up[0], "offset", turn(1))
            next_down = lax.ppermute(down[1], "offset", turn(-1))
        args = [where, shift_table, ref_image]
        specs = [scalars, scalars, whole]
        if first:
            args.append(touched)
            specs.append(whole)
        for r in needed(call):
            args += tiles[r]
            specs += [whole, whole]
        aliases = {}
        if not first:
            aliases = {len(args): 0}
            args.append(image)
            specs.append(anywhere)
        sums = [(depth, m + 2 * HMAX, LANES) for _, _, m in call for _ in range(2)]
        fields = [pltpu.VMEM((4 * depth, m + 2 * HMAX, LANES), f32) for _, _, m in call]
        scratch = fields + fields
        scratch += [pltpu.VMEM((local, depth, whole_tiles(m), LANES), jnp.bfloat16) for _, _, m in call]
        scratch += [pltpu.SemaphoreType.DMA((len(call), local // GROUP))]
        if last:
            args += done
            specs += [whole] * len(done)
            scratch = [pltpu.VMEM(dims, f32) for dims in sums] + scratch
            scratch += [pltpu.VMEM((depth, all_rows + 2 * HMAX, LANES), f32)] * 2
            half_strip = shape((n_off * 4, LANES), f32)
            outs = [shape((n_off, depth * rows, LANES), f32), half_strip, half_strip]
        else:
            outs = [shape(dims, f32) for dims in sums]
        image, *rest = pl.pallas_call(
            functools.partial(image_kernel, call, first, last),
            in_specs=specs,
            out_specs=[anywhere] + [whole] * len(outs),
            out_shape=[shape(ref_image.shape, jnp.bfloat16)] + outs,
            scratch_shapes=scratch,
            input_output_aliases=aliases,
            compiler_params=pltpu.CompilerParams(vmem_limit_bytes=16 * 2**20),
            cost_estimate=pl.CostEstimate(
                flops=20_000_000, bytes_accessed=8_000_000, transcendentals=0
            ),
            name="image",
        )(*args)
        done += rest
        if not last:
            up, down, image = lax.optimization_barrier((next_up, next_down, image))
            if at < 2:
                tiles[at + 2], tiles[6 - at] = (up[0], up[1]), (down[0], down[1])
            else:
                tiles[4] = (up, down)

    core, send_in, send_out = rest
    got_in = lax.ppermute(send_in, "space", inner_x)
    got_out = lax.ppermute(send_out, "space", outer_x)
    parts = pl.pallas_call(
        merge_kernel,
        in_specs=[scalars] + [whole] * 3,
        out_shape=shape(core.shape, f32),
        name="merge", compiler_params=SMALL,
    )(where, core, got_in, got_out)
    parts = lax.all_to_all(parts, "offset", 0, 0)
    adjoint = pl.pallas_call(
        total_kernel, out_shape=shape((depth, rows, cols), f32), name="total", compiler_params=SMALL
    )(parts)
    return image, adjoint


def solution(mesh):
    field = P(None, "offset", "space")
    in_specs = (field,) * 5 + (P("offset", None), P("offset", None, None, "space"))
    out_specs = (P("offset", None, None, "space"), field)
    return jax.shard_map(
        on_device, mesh=mesh, in_specs=in_specs, out_specs=out_specs, check_vma=False
    )
```
